32 devices in a mesh: bucket: 16 (over z, y, x), seq: 2 (over core).
Axes of the slice: x: 2, y: 2, z: 4, core: 2. Of those that a mesh axis runs over, the one named last changes fastest.
Arguments:
- tokens: bfloat16 [64, 512, 384], P('bucket', 'seq'), may hold values from -6 to 6
- cotangent: bfloat16 [64, 512, 384], P('bucket', 'seq'), may hold values from -6 to 6
- segment_ids: int32 [64, 512], P('bucket'), may hold values from 0 to 7, never falling along the last dimension, each value on 1 to 256 neighbouring positions
- pad_counts: int32 [64], P('bucket'), may hold values from 0 to 128
- timesteps: int32 [64, 8], P('bucket'), may hold values from 0 to 999
- classes: int32 [64, 8], P('bucket'), may hold values from 0 to 999
- head_mask: int32 [64, 8, 6], P('bucket'), may hold values 0 or 1
- channel_mask: int32 [64, 8, 24], P('bucket'), may hold values 0 or 1
- keep_mask: int32 [64, 512], P('bucket', 'seq'), may hold values 0 or 1
- class_table: bfloat16 [1000, 384], replicated, may hold values from -6 to 6
- w_ada: bfloat16 [384, 2304], P('bucket', 'seq'), may hold values from -0.3125 to 0.3125
- b_ada: bfloat16 [2304], P('seq'), may hold values from -2 to 2
- w_qkv: bfloat16 [384, 1152], replicated, may hold values from -0.3125 to 0.3125
- bias_qv: bfloat16 [768], replicated, may hold values from -2 to 2
- w_proj: bfloat16 [384, 384], replicated, may hold values from -2.5 to 2.5
- b_proj: bfloat16 [384], replicated, may hold values from -2 to 2
- w_fc1: bfloat16 [384, 1536], replicated, may hold values from -0.3125 to 0.3125
- b_fc1: bfloat16 [1536], replicated, may hold values from -2 to 2
- w_fc2: bfloat16 [1536, 384], replicated, may hold values from -0.15625 to 0.15625
- b_fc2: bfloat16 [384], replicated, may hold values from -2 to 2
- w_router: bfloat16 [384], replicated, may hold values from -0.3125 to 0.3125
Outputs:
- output: bfloat16 [64, 512, 384], P('bucket', 'seq')
- grad_tokens: bfloat16 [64, 512, 384], P('bucket', 'seq')
- grad_class_table: float32 [1000, 384], P(None, 'bucket')
- grad_w_ada: float32 [384, 2304], P('bucket', 'seq')
- grad_b_ada: float32 [2, 1152], P('seq', 'bucket')
- grad_w_qkv: float32 [384, 1152], P(None, 'bucket')
- grad_bias_qv: float32 [768], P('bucket')
- grad_w_proj: float32 [384, 384], P(None, 'bucket')
- grad_b_proj: float32 [384], P('bucket')
- grad_w_fc1: float32 [384, 1536], P(None, 'bucket')
- grad_b_fc1: float32 [1536], P('bucket')
- grad_w_fc2: float32 [1536, 384], P('bucket')
- grad_b_fc2: float32 [384], P('bucket')
- grad_w_router: float32 [384], P('bucket')
The draws below stay inside these ranges and needn't reach their ends.
Inputs may be any that keep to these rules, and one draw needn't show every extreme that they name: `segment_ids`: crop numbers never fall along a row; each crop has 1 to 256 tokens and one has exactly 256. The padding tokens are the last pad_counts[r] tokens of row r.
All inputs are finite; a program needn't handle non-finite values. No bound on the sum of `head_mask` or of `channel_mask` or of `keep_mask` on one device may be relied on, other than what follows from the above.
Results may differ from the reference program's by a relative error of at most 0.014.
The reference program's roundings to bfloat16 on the way count: a program that leaves them out, or rounds other values in their place, can miss the bound.
Values may be sent and summed in bfloat16 or wider, within the bound.
No kernel may reach another device: no remote copies, remote signals or barrier semaphores. Data moves between devices by JAX's collectives and lax.ppermute only.
A program may use at most 192 MiB of HBM per device.

```python
import math
import jax
import jax.numpy as jnp
import numpy as np
from jax import lax

D = 384
HEADS = 6
HEAD_DIM = 64
FF = 1536
NCLASS = 1000
CGROUPS = 24
CROPS = 8
ROWS_DEV = 4
LEN = 512
ROWS = 64
CROP_MOST = 256
PAD_MOST = 128
N_BUCKET = 16
N_SEQ = 2


def place_ends(values, key, low, top_value):
    spot = [jax.random.randint(jax.random.fold_in(key, axis), (), 0, length) for axis, length in enumerate(values.shape)]
    longest = values.shape.index(max(values.shape))
    next_to = spot[:longest] + [(spot[longest] + 1) % values.shape[longest]] + spot[longest + 1:]
    return values.at[tuple(spot)].set(low).at[tuple(next_to)].set(top_value)


def level_of(key, dims, cuts, least, high):
    def one(dim, shards_of):
        draws = jax.random.uniform(jax.random.fold_in(jax.random.fold_in(key, 6), dim), (shards_of,), jnp.float32, least / len(cuts), high / len(cuts))
        return jnp.repeat(jnp.exp(draws), dims[dim] // shards_of).reshape((-1,) + (1,) * (len(dims) - dim - 1))

    level = one(*cuts[0])
    for cut in cuts[1:]:
        level = level * one(*cut)
    return level


def length_profile(count, total, reach, lean):
    loads = [(1 << 20) // math.isqrt(rank ** lean) + 1 for rank in range(2, count + 1)]
    spare, holding = total - reach - (count - 1), [1] * (count - 1)
    while spare > 0:
        movable = [i for i in range(count - 1) if holding[i] < reach]
        mass, budget = sum([loads[i] for i in movable]), spare
        for i in movable:
            extra = min(reach - holding[i], max(1, budget * loads[i] // mass), spare)
            holding[i] = holding[i] + extra
            spare = spare - extra
    return np.array([reach] + holding)


def ragged(own_key, amount, total, bound, lean):
    if amount == 2:
        one = jax.random.randint(own_key, (), max(1, total - bound), min(bound, total - 1) + 1)
        return jnp.stack([one, total - one])
    sizes = jnp.asarray(length_profile(amount, total, bound, lean), jnp.int32)
    twos = (amount - 1) // 2
    giver, taker = sizes[1:1 + 2 * twos:2], sizes[2:2 + 2 * twos:2]
    room = jnp.minimum(giver - 1, bound - taker)
    moved = jax.random.randint(jax.random.fold_in(own_key, 1), (twos,), 0, 1 << 20) % (room + 1)
    sizes = sizes.at[1:1 + 2 * twos:2].set(giver - moved).at[2:2 + 2 * twos:2].set(taker + moved)
    return sizes[jax.random.permutation(jax.random.fold_in(own_key, 2), amount)]


def normal_values(own_key, dims, scale, bound, cuts=(), kind=jnp.bfloat16):
    values = scale * jax.random.normal(own_key, dims, jnp.float32)
    if cuts:
        values = values * level_of(own_key, dims, cuts, -0.22, 0.18)
    return jnp.clip(values, -bound, bound).astype(kind)


def setup_inputs(seed: int = 0) -> dict:
    key_of = jax.random.split(jax.random.key(seed), 22)
    tokens = normal_values(key_of[0], (ROWS, LEN, D), 1.0, 6.0, ((0, 16), (1, 2)))
    cotangent = normal_values(key_of[1], (ROWS, LEN, D), 1.0, 6.0, ((0, 16), (1, 2)))
    segment_ids = jax.vmap(lambda own: jnp.searchsorted(jnp.cumsum(ragged(own, CROPS, LEN, CROP_MOST, 1)), jnp.arange(LEN), side="right"))(jax.random.split(key_of[2], ROWS)).reshape((ROWS, LEN)).astype(jnp.int32)
    pad_counts = place_ends(jax.random.randint(key_of[3], (ROWS,), 0, PAD_MOST + 1), jax.random.fold_in(key_of[3], 1), 0, PAD_MOST).astype(jnp.int32)
    timesteps = place_ends(jax.random.randint(key_of[4], (ROWS, CROPS), 0, 1000), jax.random.fold_in(key_of[4], 1), 0, 999).astype(jnp.int32)
    classes = place_ends(jax.random.randint(key_of[5], (ROWS, CROPS), 0, NCLASS), jax.random.fold_in(key_of[5], 1), 0, NCLASS - 1).astype(jnp.int32)
    head_mask = place_ends((jax.random.randint(key_of[6], (ROWS, CROPS, HEADS), 0, 4) < 3).astype(jnp.int32), jax.random.fold_in(key_of[6], 1), 0, 1)
    channel_mask = place_ends((jax.random.randint(key_of[7], (ROWS, CROPS, CGROUPS), 0, 4) < 3).astype(jnp.int32), jax.random.fold_in(key_of[7], 1), 0, 1)
    keep_mask = place_ends((jax.random.randint(key_of[8], (ROWS, LEN), 0, 4) < 3).astype(jnp.int32), jax.random.fold_in(key_of[8], 1), 0, 1)
    class_table = normal_values(key_of[9], (NCLASS, D), 1.0, 6.0)
    w_ada = normal_values(key_of[10], (D, 6 * D), D ** -0.5, 0.3125, ((0, 16), (1, 2)))
    b_ada = normal_values(key_of[11], (6 * D,), 0.3, 2.0, ((0, 2),))
    w_qkv = normal_values(key_of[12], (D, 3 * D), D ** -0.5, 0.3125)
    bias_qv = normal_values(key_of[13], (2 * D,), 0.3, 2.0)
    w_proj = normal_values(key_of[14], (D, D), (D // 64) ** -0.5, 2.5)
    b_proj = normal_values(key_of[15], (D,), 0.3, 2.0)
    w_fc1 = normal_values(key_of[16], (D, FF), D ** -0.5, 0.3125)
    b_fc1 = normal_values(key_of[17], (FF,), 0.3, 2.0)
    w_fc2 = normal_values(key_of[18], (FF, D), FF ** -0.5, 0.15625)
    b_fc2 = normal_values(key_of[19], (D,), 0.3, 2.0)
    w_router = normal_values(key_of[20], (D,), D ** -0.5, 0.3125)
    return dict(tokens=tokens, cotangent=cotangent, segment_ids=segment_ids, pad_counts=pad_counts, timesteps=timesteps, classes=classes, head_mask=head_mask, channel_mask=channel_mask, keep_mask=keep_mask, class_table=class_table, w_ada=w_ada, b_ada=b_ada, w_qkv=w_qkv, bias_qv=bias_qv, w_proj=w_proj, b_proj=b_proj, w_fc1=w_fc1, b_fc1=b_fc1, w_fc2=w_fc2, b_fc2=b_fc2, w_router=w_router)


HIGHEST_PRECISION = lax.Precision.HIGHEST
EPSILON = 1e-06
NEGATIVE = -1e+30

@jax.custom_vjp
def low(v):
    return lax.optimization_barrier(v.astype(jnp.bfloat16)).astype(jnp.float32)

@jax.custom_vjp
def low_back(v):
    return v

def low_keep(v):
    return (low(v), None)

def low_pass(kept, grad):
    return (grad,)

def back_keep(v):
    return (v, None)

def back_low(kept, grad):
    return (low(grad),)
low.defvjp(low_keep, low_pass)
low_back.defvjp(back_keep, back_low)

def product(form, left, right):
    return jnp.einsum(form, left, right, precision=HIGHEST_PRECISION)

def layer_norm(values_in):
    centred = values_in - lax.optimization_barrier(jnp.mean(values_in, -1, keepdims=True))
    variance = lax.optimization_barrier(jnp.mean(centred * centred, -1, keepdims=True))
    return centred * lax.rsqrt(variance + EPSILON)

def time_embed(timesteps):
    half_width = D // 2
    frequency = jnp.exp(-math.log(10000.0) * jnp.arange(half_width, dtype=jnp.float32) / half_width)
    angles = timesteps.astype(jnp.float32)[..., None] * frequency
    return jnp.concatenate([jnp.cos(angles), jnp.sin(angles)], -1)

def group_forward(x_in, params, segments, pad_count, timesteps, classes, head_mask, channel_mask, keep_mask):
    class_table, w_ada, b_ada, w_qkv, bias_qv, w_proj, b_proj, w_fc1, b_fc1, w_fc2, b_fc2, w_router = params
    row_count, length, width_all = x_in.shape
    position = jnp.arange(length, dtype=jnp.int32)
    live_mask = position[None, :] < (length - pad_count)[:, None]
    live_float = live_mask.astype(jnp.float32)
    attend_ids = jnp.where(live_mask, segments, -1)
    crop_hot = (segments[:, :, None] == jnp.arange(CROPS, dtype=jnp.int32)).astype(jnp.float32)
    class_hot = (classes[:, :, None] == jnp.arange(NCLASS, dtype=jnp.int32)).astype(jnp.float32)
    condition = time_embed(timesteps) + product('rcn,nd->rcd', class_hot, class_table)
    modulation = low_back(product('rcd,dm->rcm', low(jax.nn.silu(condition)), w_ada) + b_ada)
    per_token = product('rlc,rcm->rlm', crop_hot, modulation)
    shift_one, scale_one, gate_one, shift_two, scale_two, gate_two = jnp.split(per_token, 6, axis=-1)
    hidden_one = low(layer_norm(x_in) * (1.0 + scale_one) + shift_one)
    projected = product('rld,de->rle', hidden_one, w_qkv)
    query = low(low_back(projected[..., :D] + bias_qv[:D]))
    key_all = low(low_back(projected[..., D:2 * D]))
    value_all = low(low_back(projected[..., 2 * D:] + bias_qv[D:]))

    def heads_view(matrix):
        return matrix.reshape(length, HEADS, HEAD_DIM)

    def attend_row(item):
        query_row, key_row, value_row, ids_row = item
        raw_scores = product('qhe,khe->hqk', heads_view(query_row), heads_view(key_row)) * HEAD_DIM ** (-0.5)
        same_crop = ids_row[:, None] == ids_row[None, :]
        raw_scores = low_back(jnp.where(same_crop[None], raw_scores, NEGATIVE))
        row_max = lax.optimization_barrier(jnp.max(raw_scores, -1, keepdims=True))
        numerator = jnp.exp(raw_scores - row_max)
        probability = numerator / lax.optimization_barrier(jnp.sum(numerator, -1, keepdims=True))
        mixed_heads = product('hqk,khe->qhe', low(probability), heads_view(value_row))
        return mixed_heads.reshape(length, D)
    mixed_all = lax.map(jax.checkpoint(attend_row), (query, key_all, value_all, attend_ids))
    heads_tok = product('rlc,rch->rlh', crop_hot, head_mask.astype(jnp.float32))
    attended = low(low_back(mixed_all * jnp.repeat(heads_tok, HEAD_DIM, axis=-1)))
    branch = low_back(product('rld,de->rle', attended, w_proj) + b_proj)
    residual = x_in + live_float[..., None] * gate_one * branch
    hidden_two = low(layer_norm(residual) * (1.0 + scale_two) + shift_two)
    router_rate = jax.nn.sigmoid(product('rld,d->rl', hidden_two, w_router))
    pre_act = low_back(product('rld,df->rlf', hidden_two, w_fc1) + b_fc1)
    chans_tok = product('rlc,rcf->rlf', crop_hot, jnp.repeat(channel_mask.astype(jnp.float32), FF // CGROUPS, axis=-1))
    activation = low(jax.nn.gelu(pre_act, approximate=True) * chans_tok)
    mlp_out = low_back(product('rlf,fd->rld', activation, w_fc2) + b_fc2)
    branch_coef = live_float * keep_mask.astype(jnp.float32) * router_rate
    return residual + branch_coef[..., None] * gate_two * mlp_out

def reference(tokens, cotangent, segment_ids, pad_counts, timesteps, classes, head_mask, channel_mask, keep_mask, class_table, w_ada, b_ada, w_qkv, bias_qv, w_proj, b_proj, w_fc1, b_fc1, w_fc2, b_fc2, w_router):
    weights = tuple((weight.astype(jnp.float32) for weight in (class_table, w_ada, b_ada, w_qkv, bias_qv, w_proj, b_proj, w_fc1, b_fc1, w_fc2, b_fc2, w_router)))

    def grouped(array):
        return array.reshape((N_BUCKET, ROWS_DEV) + array.shape[1:])
    items = tuple((grouped(array) for array in (tokens, cotangent, segment_ids, pad_counts, timesteps, classes, head_mask, channel_mask, keep_mask)))

    def step_group(totals, item):
        x_group, cot_group, segments, pad_count, times_group, class_group, heads_group, chans_group, keep_group = item

        def forward(x_in, params):
            return group_forward(x_in, params, segments, pad_count, times_group, class_group, heads_group, chans_group, keep_group)
        result, pull_back = jax.vjp(forward, x_group.astype(jnp.float32), weights)
        grad_input, grad_params = pull_back(cot_group.astype(jnp.float32))
        totals = jax.tree.map(jnp.add, totals, grad_params)
        return (totals, (result.astype(jnp.bfloat16), grad_input.astype(jnp.bfloat16)))
    zero_grads = jax.tree.map(jnp.zeros_like, weights)
    totals, (outputs, grads_input) = lax.scan(step_group, zero_grads, items)
    full_shape = tokens.shape
    return (outputs.reshape(full_shape), grads_input.reshape(full_shape), totals[0], totals[1], totals[2].reshape(N_SEQ, -1), totals[3], totals[4], totals[5], totals[6], totals[7], totals[8], totals[9], totals[10], totals[11])
```

```python
from functools import partial
import math

import jax
import jax.numpy as jnp
from jax import lax
from jax.experimental import pallas as pl
from jax.experimental.pallas import tpu as pltpu
from jax.sharding import PartitionSpec as P

D = 384
HEADS = 6
HEAD_DIM = 64
FF = 1536
NCLASS = 1000
CGROUPS = 24
CROPS = 8
EPSILON = 1e-06
NEGATIVE = -1e30
PAIR = 2 * HEAD_DIM
TOK = 256
FCH = 256
GELU_A = math.sqrt(2.0 / math.pi)
GELU_B = 0.044715
F32 = jnp.float32
BF16 = jnp.bfloat16


def dot(left, right):
    return jnp.dot(left, right, preferred_element_type=F32)


def dot_nt(left, right):
    return lax.dot_general(left, right, (((1,), (1,)), ((), ())), preferred_element_type=F32)


def dot_tn(left, right):
    return lax.dot_general(left, right, (((0,), (0,)), ((), ())), preferred_element_type=F32)


def normalise(values):
    centred = values - jnp.mean(values, -1, keepdims=True)
    inverse = lax.rsqrt(jnp.mean(centred * centred, -1, keepdims=True) + EPSILON)
    return centred * inverse, inverse


def normalise_back(grad, normal, inverse):
    return inverse * (
        grad
        - jnp.mean(grad, -1, keepdims=True)
        - normal * jnp.mean(grad * normal, -1, keepdims=True)
    )


def three_terms(values):
    high = values.astype(BF16).astype(F32)
    rest = values - high
    middle = rest.astype(BF16).astype(F32)
    last = rest - middle
    return jnp.concatenate([high, middle, last, jnp.zeros_like(last)], 0).astype(BF16)


def crop_rows(column, count):
    lane = lax.broadcasted_iota(jnp.int32, (count, 4 * CROPS), 1)
    return jnp.where((lane & (CROPS - 1)).astype(F32) == column, 1.0, 0.0).astype(BF16)


def crop_columns(row, count):
    line = lax.broadcasted_iota(jnp.int32, (2 * CROPS, count), 0).astype(F32)
    return jnp.where(line == row, 1.0, 0.0).astype(BF16)


def half_lanes(values, half):
    lane = lax.broadcasted_iota(jnp.int32, values.shape, 1)
    return jnp.where((lane // HEAD_DIM) == half, values, jnp.zeros_like(values))


def forward_kernel(
    place,
    tok_own,
    tok_in,
    cot_own,
    cot_in,
    col,
    row,
    mod,
    head_tab,
    chan_tab,
    w_qkv,
    b_qv,
    w_proj,
    b_proj,
    w_fc1,
    b_fc1,
    w_fc2,
    b_fc2,
    w_router,
    out_own,
    out_far,
    hid_out,
    q_out,
    k_out,
    v_out,
    prob_out,
    gheads_out,
    gres_out,
    dw1,
    dw2,
    dwp,
    db1,
    db2,
    dbp,
    dwr,
    gmod,
    x_s,
    cot_s,
    bias_s,
    hot_s,
    tab_s,
    mix_s,
    att_s,
    branch_s,
    res_s,
    h2_s,
    coef_s,
    gml_s,
    mlp_s,
    gh2_s,
    gm_s,
):
    length = x_s.shape[0]
    local = tok_own.shape[1]
    far = tok_in.shape[0]

    @pl.when(pl.program_id(0) == 0)
    def _():
        for ref in (dw1, dw2, dwp, db1, db2, dbp, dwr):
            ref[...] = jnp.zeros_like(ref)

    x_s[0:local] = tok_own[0].astype(F32)
    cot_s[0:local] = cot_own[0].astype(F32)
    for j in range(far):
        x_s[(j + 1) * local : (j + 2) * local] = tok_in[j, 0].astype(F32)
        cot_s[(j + 1) * local : (j + 2) * local] = cot_in[j, 0].astype(F32)
    tab_s[...] = three_terms(mod[0])
    mlp_s[...] = jnp.zeros_like(mlp_s)
    gh2_s[...] = jnp.zeros_like(gh2_s)
    gm_s[...] = jnp.zeros_like(gm_s)
    id_row = row[0, 0:1, :]

    def first(i, _):
        part = pl.ds(i * TOK, TOK)
        hot = crop_rows(col[0, part, 0:1], TOK)
        hot_s[part] = hot
        bias_s[part] = jnp.where(col[0, part, 1:2] == id_row, 0.0, NEGATIVE)
        normal, _ = normalise(x_s[part])
        hidden = (normal * (1.0 + dot(hot, tab_s[:, D : 2 * D])) + dot(hot, tab_s[:, 0:D])).astype(
            BF16
        )
        hid_out[0, part] = hidden
        q_out[0, part] = (dot(hidden, w_qkv[:, 0:D]) + b_qv[:, 0:D]).astype(BF16) * BF16(
            HEAD_DIM**-0.5
        )
        k_out[0, part] = dot(hidden, w_qkv[:, D : 2 * D]).astype(BF16)
        v_out[0, part] = (dot(hidden, w_qkv[:, 2 * D :]) + b_qv[:, D:]).astype(BF16)
        return 0

    lax.fori_loop(0, length // TOK, first, 0)

    def attend(hp, _):
        lanes = pl.ds(pl.multiple_of(hp * PAIR, PAIR), PAIR)
        query, key = q_out[0, :, lanes], k_out[0, :, lanes]
        value_t = v_out[0, :, lanes].T
        for half in range(2):
            key_half = half_lanes(key, half)
            for c in range(length // TOK):
                cols = slice(c * TOK, (c + 1) * TOK)
                scores = dot_nt(key_half, query[cols]) + bias_s[:, cols]
                top = jnp.max(scores, 0, keepdims=True)
                numerator = jnp.exp(scores - top)
                scale = 1.0 / jnp.sum(numerator, 0, keepdims=True)
                prob = (numerator * scale).astype(BF16)
                prob_out[0, 2 * hp + half, :, cols] = prob
                mix_s[half * HEAD_DIM : (half + 1) * HEAD_DIM, cols] = dot(
                    value_t[half * HEAD_DIM : (half + 1) * HEAD_DIM], prob
                )
        keep_heads = dot(hot_s[...], head_tab[0, :, lanes])
        att_s[:, lanes] = (mix_s[...].T * keep_heads).astype(BF16)
        return 0

    lax.fori_loop(0, D // PAIR, attend, 0)

    def middle(i, _):
        part = pl.ds(i * TOK, TOK)
        hot = hot_s[part]
        live = jnp.where(col[0, part, 1:2] >= 0.0, 1.0, 0.0)
        branch = dot(att_s[part], w_proj[...]) + b_proj[...]
        branch_s[part] = branch
        residual = x_s[part] + live * dot(hot, tab_s[:, 2 * D : 3 * D]) * branch
        res_s[part] = residual
        normal, _ = normalise(residual)
        hidden = (
            normal * (1.0 + dot(hot, tab_s[:, 4 * D : 5 * D])) + dot(hot, tab_s[:, 3 * D : 4 * D])
        ).astype(BF16)
        h2_s[part] = hidden
        logit = jnp.sum(hidden.astype(F32) * w_router[...], -1, keepdims=True)
        rate = 1.0 / (1.0 + jnp.exp(-logit))
        keep = live * col[0, part, 2:3]
        coef = keep * rate
        coef_s[part, 0:1] = coef
        coef_s[part, 1:2] = coef * (1.0 - rate)
        gml = (cot_s[part] * coef * dot(hot, tab_s[:, 5 * D : 6 * D])).astype(BF16)
        gml_s[part] = gml
        db2[...] += jnp.sum(gml.astype(F32), 0, keepdims=True)
        return 0

    lax.fori_loop(0, length // TOK, middle, 0)

    def feed(c, _):
        units = pl.ds(pl.multiple_of(c * FCH, FCH), FCH)
        hidden, gml = h2_s[...], gml_s[...]
        pre = dot(hidden, w_fc1[:, units]) + b_fc1[:, units]
        mask = dot(hot_s[...], chan_tab[0, :, units])
        square = pre * pre
        tanh = jnp.tanh(pre * (GELU_A + (GELU_A * GELU_B) * square))
        half = 0.5 * pre
        side = 0.5 + 0.5 * tanh
        act = (pre * side * mask).astype(BF16)
        slope = side + half * (1.0 - tanh * tanh) * (GELU_A + (3.0 * GELU_A * GELU_B) * square)
        mlp_s[...] += dot(act, w_fc2[units, :])
        dw2[units, :] += dot_tn(act, gml)
        gpre = (slope * mask * dot_nt(gml, w_fc2[units, :])).astype(BF16)
        dw1[units, :] += dot_tn(gpre, hidden)
        db1[:, units] += jnp.sum(gpre.astype(F32), 0, keepdims=True)
        gh2_s[...] += dot_nt(gpre, w_fc1[:, units])
        return 0

    lax.fori_loop(0, FF // FCH, feed, 0)

    def last(i, _):
        part = pl.ds(i * TOK, TOK)
        hot = hot_s[part]
        live = jnp.where(col[0, part, 1:2] >= 0.0, 1.0, 0.0)
        coef = coef_s[part, 0:1]
        cot = cot_s[part]
        mlp = mlp_s[part] + b_fc2[...]
        gate2 = dot(hot, tab_s[:, 5 * D : 6 * D])
        residual = res_s[part]
        outcome = (residual + coef * gate2 * mlp).astype(BF16)
        mlp_s[part] = outcome.astype(F32)
        cot_mlp = cot * mlp
        grad_logit = jnp.sum(cot_mlp * gate2, -1, keepdims=True) * coef_s[part, 1:2]
        hidden = h2_s[part].astype(F32)
        dwr[...] += jnp.sum(hidden * grad_logit, 0, keepdims=True)
        grad_hidden = gh2_s[part] + grad_logit * w_router[...]
        normal, inverse = normalise(residual)
        grad_res = cot + normalise_back(
            grad_hidden * (1.0 + dot(hot, tab_s[:, 4 * D : 5 * D])), normal, inverse
        )
        gres_out[0, part] = grad_res
        grad_live = grad_res * live
        grad_branch = (grad_live * dot(hot, tab_s[:, 2 * D : 3 * D])).astype(BF16)
        hot_t = crop_columns(row[0, 1:2, part], TOK)
        gm_s[:, 0:D] += dot(hot_t, (grad_live * branch_s[part]).astype(BF16))
        gm_s[:, D : 2 * D] += dot(hot_t, grad_hidden.astype(BF16))
        gm_s[:, 2 * D : 3 * D] += dot(hot_t, (grad_hidden * normal).astype(BF16))
        gm_s[:, 3 * D : 4 * D] += dot(hot_t, (cot_mlp * coef).astype(BF16))
        dbp[...] += jnp.sum(grad_branch.astype(F32), 0, keepdims=True)
        dwp[...] += dot_tn(grad_branch, att_s[part])
        gheads_out[0, part] = (
            dot_nt(grad_branch, w_proj[...]).astype(BF16).astype(F32) * dot(hot, head_tab[0])
        ).astype(BF16)
        return 0

    lax.fori_loop(0, length // TOK, last, 0)
    out_own[0] = mlp_s[0:local].astype(BF16)
    for j in range(far):
        out_far[j, 0] = mlp_s[(j + 1) * local : (j + 2) * local].astype(BF16)
    gmod[0] = gm_s[0:CROPS]


def backward_kernel(
    place,
    tok_own,
    tok_in,
    col,
    row,
    mod,
    w_qkv,
    hid,
    q_in,
    k_in,
    v_in,
    prob_in,
    gheads,
    gres,
    gt_own,
    gt_far,
    dwq,
    dbq,
    gmod,
    gp_s,
    dk_s,
    dv_s,
    dq_s,
    x_s,
    tab_s,
    gm_s,
):
    length = x_s.shape[0]
    local = tok_own.shape[1]
    far = tok_in.shape[0]

    @pl.when(pl.program_id(0) == 0)
    def _():
        for ref in (dwq, dbq):
            ref[...] = jnp.zeros_like(ref)

    x_s[0:local] = tok_own[0].astype(F32)
    for j in range(far):
        x_s[(j + 1) * local : (j + 2) * local] = tok_in[j, 0].astype(F32)
    tab_s[...] = three_terms(mod[0, :, D : 2 * D])
    gm_s[...] = jnp.zeros_like(gm_s)

    def attend(hp, _):
        lanes = pl.ds(pl.multiple_of(hp * PAIR, PAIR), PAIR)
        query, key, value = q_in[0, :, lanes], k_in[0, :, lanes], v_in[0, :, lanes]
        grad = gheads[0, :, lanes]
        key_t = key.T
        dk_s[...] = jnp.zeros_like(dk_s)
        dv_s[...] = jnp.zeros_like(dv_s)
        for half in range(2):
            value_half = half_lanes(value, half)
            for c in range(length // TOK):
                cols = slice(c * TOK, (c + 1) * TOK)
                prob_low = prob_in[0, 2 * hp + half, :, cols]
                prob = prob_low.astype(F32)
                grad_cols = grad[cols]
                product = prob * dot_nt(value_half, grad_cols)
                inner = jnp.sum(product, 0, keepdims=True)
                grad_scores = (product - prob * inner).astype(BF16)
                dv_s[...] += dot(prob_low, half_lanes(grad_cols, half))
                dk_s[...] += dot(grad_scores, half_lanes(query[cols], half))
                dq_s[half * HEAD_DIM : (half + 1) * HEAD_DIM, cols] = dot(
                    key_t[half * HEAD_DIM : (half + 1) * HEAD_DIM], grad_scores
                )
        gp_s[:, lanes] = (dq_s[...].T * HEAD_DIM**-0.5).astype(BF16)
        gp_s[:, pl.ds(pl.multiple_of(D + hp * PAIR, PAIR), PAIR)] = dk_s[...].astype(BF16)
        gp_s[:, pl.ds(pl.multiple_of(2 * D + hp * PAIR, PAIR), PAIR)] = dv_s[...].astype(BF16)
        return 0

    lax.fori_loop(0, D // PAIR, attend, 0)

    def last(i, _):
        part = pl.ds(i * TOK, TOK)
        hot = crop_rows(col[0, part, 0:1], TOK)
        grad = gp_s[part]
        dbq[...] += jnp.sum(grad.astype(F32), 0, keepdims=True)
        grad_hidden = dot_nt(grad, w_qkv[...])
        normal, inverse = normalise(x_s[part])
        hot_t = crop_columns(row[0, 1:2, part], TOK)
        gm_s[:, 0:D] += dot(hot_t, grad_hidden.astype(BF16))
        gm_s[:, D : 2 * D] += dot(hot_t, (grad_hidden * normal).astype(BF16))
        x_s[part] = gres[0, part] + normalise_back(
            grad_hidden * (1.0 + dot(hot, tab_s[...])), normal, inverse
        )
        return 0

    lax.fori_loop(0, length // TOK, last, 0)
    for c in range(3):
        rows = slice(c * D, (c + 1) * D)
        dwq[rows, :] += dot_tn(gp_s[:, rows], hid[0])
    gt_own[0] = x_s[0:local].astype(BF16)
    for j in range(far):
        gt_far[j, 0] = x_s[(j + 1) * local : (j + 2) * local].astype(BF16)
    gmod[0] = gm_s[0:CROPS]


def whole(shape):
    return pl.BlockSpec(shape, lambda r, place: (0,) * len(shape))


def per_row(shape):
    return pl.BlockSpec((1,) + shape, lambda r, place: (r,) + (0,) * len(shape))


def per_far(count, shape):
    return pl.BlockSpec((count, 1) + shape, lambda r, place: (0, r) + (0,) * len(shape))


def body(
    tokens,
    cotangent,
    segment_ids,
    pad_counts,
    timesteps,
    classes,
    head_mask,
    channel_mask,
    keep_mask,
    class_table,
    w_ada,
    b_ada,
    w_qkv,
    bias_qv,
    w_proj,
    b_proj,
    w_fc1,
    b_fc1,
    w_fc2,
    b_fc2,
    w_router,
):
    seqs, buckets = lax.axis_size("seq"), lax.axis_size("bucket")
    me_s, me_b = lax.axis_index("seq"), lax.axis_index("bucket")
    row_count, local, _ = tokens.shape
    mine = row_count // seqs
    length = local * seqs
    crops_here = row_count * CROPS
    crops_mine = mine * CROPS
    inner, outer = 4, buckets // 4

    def seq_hop(value, step):
        return lax.ppermute(value, "seq", [(i, i ^ step) for i in range(seqs)])

    def plane_hop(value, step):
        return lax.ppermute(value, "bucket", [(i, i ^ step) for i in range(buckets)])

    def line_hop(value, step):
        return lax.ppermute(value, "bucket", [(i, i ^ (step * inner)) for i in range(buckets)])

    def slab(value, device, count):
        return lax.dynamic_slice_in_dim(value, device * count, count, 0)

    def by_device(pieces, device):
        chosen = pieces[0]
        for j in range(1, seqs):
            chosen = jnp.where((me_s ^ device) == j, pieces[j], chosen)
        return chosen

    def deal_rows(value):
        return [seq_hop(slab(value, me_s ^ j, mine), j) for j in range(1, seqs)]

    tok_in = jnp.stack(deal_rows(tokens))
    cot_in = jnp.stack(deal_rows(cotangent))
    keep_in = deal_rows(keep_mask)

    ada_parts = [w_ada] + [line_hop(w_ada, k) for k in range(1, outer)]
    ada_line = jnp.concatenate(ada_parts, 0)
    ada_all = jnp.concatenate([ada_line] + [plane_hop(ada_line, k) for k in range(1, inner)], 0)

    position = jnp.arange(length, dtype=jnp.int32)
    live_row = position[None, :] < (length - pad_counts)[:, None]
    attend_ids = jnp.where(live_row, segment_ids, -1)
    both = jnp.stack([segment_ids, attend_ids]).astype(F32)
    both = lax.dynamic_slice_in_dim(both, me_s * mine, mine, 1)
    both = jnp.concatenate(
        [lax.dynamic_slice_in_dim(both, (me_s ^ j) * local, local, 2) for j in range(seqs)], 2
    )
    keep_all = jnp.concatenate([slab(keep_mask, me_s, mine)] + keep_in, 1).astype(F32)
    col = jnp.stack([both[0], both[1], keep_all, keep_all], -1)
    row = jnp.stack([both[1], both[0]], 1)

    half_width = D // 2
    frequency = jnp.exp(-math.log(10000.0) * jnp.arange(half_width, dtype=F32) / half_width)
    angles = timesteps.reshape(crops_here, 1).astype(F32) * frequency
    class_ids = classes.reshape(crops_here)
    class_hot = (class_ids[:, None] == jnp.arange(NCLASS, dtype=jnp.int32)).astype(BF16)
    condition = jnp.concatenate([jnp.cos(angles), jnp.sin(angles)], -1) + dot(
        class_hot, class_table
    )
    sigmoid = 1.0 / (1.0 + jnp.exp(-condition))
    silu_low = (condition * sigmoid).astype(BF16)
    silu_slope = sigmoid * (1.0 + condition * (1.0 - sigmoid))
    near = jnp.arange(buckets)
    order = me_b ^ ((near // outer) + inner * (near % outer))
    depth = D // buckets
    silu_near = jnp.take(silu_low.reshape(crops_here, buckets, depth), order, axis=1).reshape(
        crops_here, D
    )
    slope_near = jnp.take(silu_slope.reshape(crops_here, buckets, depth), order, axis=1).reshape(
        crops_here, D
    )
    mod_part = dot(silu_near, ada_all) + b_ada.astype(F32)
    mod_pieces = [slab(mod_part, me_s, crops_mine)] + deal_rows_of(mod_part, seqs, me_s, crops_mine)
    modulation = jnp.concatenate([by_device(mod_pieces, d) for d in range(seqs)], 1).reshape(
        mine, CROPS, 6 * D
    )

    def table_of(mask, width):
        wide = jnp.repeat(mask, width, axis=-1).astype(BF16)
        return jnp.pad(wide, ((0, 0), (0, 3 * CROPS), (0, 0)))

    head_tab = table_of(slab(head_mask, me_s, mine), HEAD_DIM)
    chan_tab = table_of(slab(channel_mask, me_s, mine), FF // CGROUPS)
    place = me_s.reshape(1).astype(jnp.int32)
    own = pl.BlockSpec((1, local, D), lambda r, place: (place[0] * mine + r, 0, 0))
    far = seqs - 1
    bias_row = bias_qv.astype(F32).reshape(1, 2 * D)

    def struct(shape, kind=F32):
        return jax.ShapeDtypeStruct(shape, kind)

    fwd_shapes = [
        struct((mine, local, D), BF16),
        struct((far, mine, local, D), BF16),
        struct((mine, length, D), BF16),
        struct((mine, length, D), BF16),
        struct((mine, length, D), BF16),
        struct((mine, length, D), BF16),
        struct((mine, HEADS, length, length), BF16),
        struct((mine, length, D), BF16),
        struct((mine, length, D)),
        struct((FF, D)),
        struct((FF, D)),
        struct((D, D)),
        struct((1, FF)),
        struct((1, D)),
        struct((1, D)),
        struct((1, D)),
        struct((mine, CROPS, 4 * D)),
    ]
    fwd_out_specs = [
        per_row((local, D)),
        per_far(far, (local, D)),
        per_row((length, D)),
        per_row((length, D)),
        per_row((length, D)),
        per_row((length, D)),
        per_row((HEADS, length, length)),
        per_row((length, D)),
        per_row((length, D)),
        whole((FF, D)),
        whole((FF, D)),
        whole((D, D)),
        whole((1, FF)),
        whole((1, D)),
        whole((1, D)),
        whole((1, D)),
        per_row((CROPS, 4 * D)),
    ]
    tokens_here = mine * length
    (
        out_own,
        out_far,
        hid,
        query,
        key,
        value,
        prob,
        grad_heads,
        grad_res,
        dw1,
        dw2,
        dwp,
        db1,
        db2,
        dbp,
        dwr,
        gmod_late,
    ) = pl.pallas_call(
        forward_kernel,
        grid_spec=pltpu.PrefetchScalarGridSpec(
            num_scalar_prefetch=1,
            grid=(mine,),
            in_specs=[
                own,
                per_far(far, (local, D)),
                own,
                per_far(far, (local, D)),
                per_row((length, 4)),
                per_row((2, length)),
                per_row((CROPS, 6 * D)),
                per_row((4 * CROPS, D)),
                per_row((4 * CROPS, FF)),
                whole((D, 3 * D)),
                whole((1, 2 * D)),
                whole((D, D)),
                whole((1, D)),
                whole((D, FF)),
                whole((1, FF)),
                whole((FF, D)),
                whole((1, D)),
                whole((1, D)),
            ],
            out_specs=fwd_out_specs,
            scratch_shapes=[
                pltpu.VMEM((length, D), F32),
                pltpu.VMEM((length, D), F32),
                pltpu.VMEM((length, length), F32),
                pltpu.VMEM((length, 4 * CROPS), BF16),
                pltpu.VMEM((4 * CROPS, 6 * D), BF16),
                pltpu.VMEM((PAIR, length), F32),
                pltpu.VMEM((length, D), BF16),
                pltpu.VMEM((length, D), F32),
                pltpu.VMEM((length, D), F32),
                pltpu.VMEM((length, D), BF16),
                pltpu.VMEM((length, 2), F32),
                pltpu.VMEM((length, D), BF16),
                pltpu.VMEM((length, D), F32),
                pltpu.VMEM((length, D), F32),
                pltpu.VMEM((2 * CROPS, 4 * D), F32),
            ],
        ),
        out_shape=fwd_shapes,
        cost_estimate=pl.CostEstimate(
            flops=2 * tokens_here * (4 * D * D + 6 * D * FF + 2 * D * length),
            transcendentals=tokens_here * (FF + HEADS * length),
            bytes_accessed=20_000_000,
        ),
    )(
        place,
        tokens,
        tok_in,
        cotangent,
        cot_in,
        col,
        row,
        modulation,
        head_tab,
        chan_tab,
        w_qkv,
        bias_row,
        w_proj,
        b_proj.astype(F32).reshape(1, D),
        w_fc1,
        b_fc1.astype(F32).reshape(1, FF),
        w_fc2,
        b_fc2.astype(F32).reshape(1, D),
        w_router.astype(F32).reshape(1, D),
    )

    def return_rows(own_piece, far_pieces):
        pieces = [own_piece] + [seq_hop(far_pieces[j - 1], j) for j in range(1, seqs)]
        return jnp.concatenate([by_device(pieces, d) for d in range(seqs)], 0)

    def sum_over_all(parts):
        joined = jnp.concatenate([part.reshape(buckets, -1, D) for part in parts], 1)
        lines = joined.shape[1] // seqs
        joined = joined.reshape(buckets, seqs, lines, D)
        joined = jnp.take(joined, order, axis=0)
        total = lax.dynamic_index_in_dim(joined, me_s, 1, keepdims=False)
        for j in range(1, seqs):
            sent = lax.dynamic_index_in_dim(joined, me_s ^ j, 1, keepdims=False).astype(BF16)
            total = total + seq_hop(sent, j).astype(F32)
        total = sum_over_buckets(total)
        pieces = [total] + [seq_hop(total, j) for j in range(1, seqs)]
        return jnp.concatenate([by_device(pieces, d) for d in range(seqs)], 0)

    def sum_over_buckets(total):
        total = total.reshape((inner, outer) + total.shape[1:])
        plane = total[0]
        low = total.astype(BF16)
        for k in range(1, inner):
            plane = plane + plane_hop(low[k], k).astype(F32)
        line = plane[0]
        low = plane.astype(BF16)
        for k in range(1, outer):
            line = line + line_hop(low[k], k).astype(F32)
        return line

    output = return_rows(out_own, out_far)
    early = sum_over_all([dw1, dw2])

    gt_own, gt_far, dwq, dbq, gmod_first = pl.pallas_call(
        backward_kernel,
        grid_spec=pltpu.PrefetchScalarGridSpec(
            num_scalar_prefetch=1,
            grid=(mine,),
            in_specs=[
                own,
                per_far(far, (local, D)),
                per_row((length, 4)),
                per_row((2, length)),
                per_row((CROPS, 6 * D)),
                whole((D, 3 * D)),
                per_row((length, D)),
                per_row((length, D)),
                per_row((length, D)),
                per_row((length, D)),
                per_row((HEADS, length, length)),
                per_row((length, D)),
                per_row((length, D)),
            ],
            out_specs=[
                per_row((local, D)),
                per_far(far, (local, D)),
                whole((3 * D, D)),
                whole((1, 3 * D)),
                per_row((CROPS, 2 * D)),
            ],
            scratch_shapes=[
                pltpu.VMEM((length, 3 * D), BF16),
                pltpu.VMEM((length, PAIR), F32),
                pltpu.VMEM((length, PAIR), F32),
                pltpu.VMEM((PAIR, length), F32),
                pltpu.VMEM((length, D), F32),
                pltpu.VMEM((4 * CROPS, D), BF16),
                pltpu.VMEM((2 * CROPS, 2 * D), F32),
            ],
        ),
        out_shape=[
            struct((mine, local, D), BF16),
            struct((far, mine, local, D), BF16),
            struct((3 * D, D)),
            struct((1, 3 * D)),
            struct((mine, CROPS, 2 * D)),
        ],
        cost_estimate=pl.CostEstimate(
            flops=2 * tokens_here * (6 * D * D + 5 * D * length),
            transcendentals=0,
            bytes_accessed=20_000_000,
        ),
    )(
        place,
        tokens,
        tok_in,
        col,
        row,
        modulation,
        w_qkv,
        hid,
        query,
        key,
        value,
        prob,
        grad_heads,
        grad_res,
    )
    grad_tokens = return_rows(gt_own, gt_far)
    late = sum_over_all([dwq, dwp])

    grad_mod = jnp.concatenate([gmod_first, gmod_late], -1).astype(BF16).reshape(crops_mine, 6 * D)
    width = 6 * D // seqs
    mod_pieces = [lax.dynamic_slice_in_dim(grad_mod, me_s * width, width, 1)] + [
        seq_hop(lax.dynamic_slice_in_dim(grad_mod, (me_s ^ j) * width, width, 1), j)
        for j in range(1, seqs)
    ]
    grad_mod = jnp.concatenate([by_device(mod_pieces, d) for d in range(seqs)], 0)
    grad_w_ada = sum_over_buckets(
        lax.dot_general(
            silu_near, grad_mod, (((0,), (0,)), ((), ())), preferred_element_type=F32
        ).reshape(buckets, depth, width)
    )

    grad_b_ada = jnp.sum(grad_mod.astype(F32), 0).reshape(buckets, -1)
    grad_silu = dot_nt(grad_mod, ada_all)
    small = jnp.concatenate(
        [
            part.reshape(buckets, -1)
            for part in (
                db1,
                db2,
                dbp,
                dwr,
                jnp.concatenate([dbq[:, 0:D], dbq[:, 2 * D :]], 1),
            )
        ],
        1,
    )
    small_size = small.shape[1]
    for j in [1 << b for b in range(seqs.bit_length() - 1)]:
        grad_silu = grad_silu + seq_hop(grad_silu, j)
        small = small + seq_hop(small, j)
    grad_condition = grad_silu * slope_near
    crop_part = grad_condition.reshape(crops_here, buckets, depth).swapaxes(0, 1)
    parcel = jnp.concatenate(
        [
            crop_part.reshape(buckets, crops_here * depth),
            jnp.take(small, order, axis=0),
            jnp.take(grad_b_ada, order, axis=0),
            jnp.broadcast_to(class_ids.astype(F32)[None], (buckets, crops_here)),
        ],
        1,
    ).reshape(inner, outer, -1)
    parcel = jnp.stack([parcel[0]] + [plane_hop(parcel[k], k) for k in range(1, inner)])
    parcel = jnp.stack([parcel[:, 0]] + [line_hop(parcel[:, k], k) for k in range(1, outer)])
    parcel = parcel.reshape(buckets, -1)
    first = crops_here * depth
    crop_grads = parcel[:, :first].reshape(buckets * crops_here, depth)
    small = jnp.sum(parcel[:, first : first + small_size + grad_b_ada.shape[1]], 0)
    source_ids = parcel[:, first + small_size + grad_b_ada.shape[1] :].reshape(1, -1)
    hot = (jnp.arange(NCLASS, dtype=F32)[:, None] == source_ids).astype(F32)
    grad_table = jnp.dot(hot, crop_grads, precision=lax.Precision.HIGHEST)

    ff_part, d_part = FF // buckets, D // buckets
    cuts = [0]
    for size in (ff_part, d_part, d_part, d_part, 2 * d_part, grad_b_ada.shape[1]):
        cuts.append(cuts[-1] + size)
    v_b1, v_b2, v_bp, v_wr, v_qv, v_ada = (small[a:b] for a, b in zip(cuts[:-1], cuts[1:]))
    return (
        output,
        grad_tokens,
        grad_table,
        grad_w_ada,
        v_ada.reshape(1, -1),
        late[: 3 * d_part].T,
        v_qv,
        late[3 * d_part :].T,
        v_bp,
        early[:ff_part].T,
        v_b1,
        early[ff_part:],
        v_b2,
        v_wr,
    )


def deal_rows_of(value, seqs, me_s, count):
    return [
        lax.ppermute(
            lax.dynamic_slice_in_dim(value, (me_s ^ j) * count, count, 0),
            "seq",
            [(i, i ^ j) for i in range(seqs)],
        )
        for j in range(1, seqs)
    ]


def solution(mesh):
    placed = (
        P("bucket", "seq", None),
        P("bucket", "seq", None),
        P("bucket", None),
        P("bucket"),
        P("bucket", None),
        P("bucket", None),
        P("bucket", None, None),
        P("bucket", None, None),
        P("bucket", "seq"),
        P(),
        P("bucket", "seq"),
        P("seq"),
        P(),
        P(),
        P(),
        P(),
        P(),
        P(),
        P(),
        P(),
        P(),
    )
    return jax.shard_map(
        body,
        mesh=mesh,
        in_specs=placed,
        out_specs=(
            P("bucket", "seq", None),
            P("bucket", "seq", None),
            P(None, "bucket"),
            P("bucket", "seq"),
            P("seq", "bucket"),
            P(None, "bucket"),
            P("bucket"),
            P(None, "bucket"),
            P("bucket"),
            P(None, "bucket"),
            P("bucket"),
            P("bucket", None),
            P("bucket"),
            P("bucket"),
        ),
        check_vma=False,
    )
```

```python
from functools import partial
import math

import jax
import jax.numpy as jnp
from jax import lax
from jax.experimental import pallas as pl
from jax.experimental.pallas import tpu as pltpu
from jax.sharding import PartitionSpec as P

D = 384
HEADS = 6
HEAD_DIM = 64
FF = 1536
NCLASS = 1000
CGROUPS = 24
CROPS = 8
EPSILON = 1e-06
NEGATIVE = -1e30
PAIR = 2 * HEAD_DIM
TOK = 256
FCH = 256
LANES = 128
INNER = 4
GELU_A = math.sqrt(2.0 / math.pi)
GELU_B = 0.044715
F32 = jnp.float32
BF16 = jnp.bfloat16


def dot(left, right):
    return jnp.dot(left, right, preferred_element_type=F32)


def dot_nt(left, right):
    return lax.dot_general(left, right, (((1,), (1,)), ((), ())), preferred_element_type=F32)


def dot_tn(left, right):
    return lax.dot_general(left, right, (((0,), (0,)), ((), ())), preferred_element_type=F32)


def normalise(values):
    centred = values - jnp.mean(values, -1, keepdims=True)
    inverse = lax.rsqrt(jnp.mean(centred * centred, -1, keepdims=True) + EPSILON)
    return centred * inverse, inverse


def normalise_back(grad, normal, inverse):
    return inverse * (
        grad
        - jnp.mean(grad, -1, keepdims=True)
        - normal * jnp.mean(grad * normal, -1, keepdims=True)
    )


def three_terms(values):
    high = values.astype(BF16).astype(F32)
    rest = values - high
    middle = rest.astype(BF16).astype(F32)
    last = rest - middle
    return jnp.concatenate([high, middle, last, jnp.zeros_like(last)], 0).astype(BF16)


def crop_rows(column, count):
    lane = lax.broadcasted_iota(jnp.int32, (count, 4 * CROPS), 1)
    return jnp.where((lane & (CROPS - 1)).astype(F32) == column, 1.0, 0.0).astype(BF16)


def crop_columns(row, count):
    line = lax.broadcasted_iota(jnp.int32, (2 * CROPS, count), 0).astype(F32)
    return jnp.where(line == row, 1.0, 0.0).astype(BF16)


def half_lanes(values, half):
    lane = lax.broadcasted_iota(jnp.int32, values.shape, 1)
    return jnp.where((lane // HEAD_DIM) == half, values, jnp.zeros_like(values))


FWD_IN = (
    "place",
    "tok_own",
    "tok_in",
    "cot_own",
    "cot_in",
    "row",
    "mod",
    "head_tab",
    "chan_tab",
    "w_qkv",
    "b_qv",
    "w_proj",
    "b_proj",
    "w_fc1",
    "b_fc1",
    "w_fc2",
    "b_fc2",
    "w_router",
)
FWD_OUT = (
    "out_own",
    "out_far",
    "hid_out",
    "q_out",
    "k_out",
    "v_out",
    "prob_out",
    "gheads_out",
    "gres_out",
    "dwp",
    "gmod",
)
FWD_FAST = ("e_own", "e_send", "parcel", "gme_own", "gme_send")
FWD_SUMS = ("dw1", "dw2", "db2", "dwr")
FWD_TEMP = (
    "x_s",
    "cot_s",
    "bias_s",
    "hot_s",
    "tab_s",
    "mix_s",
    "att_s",
    "branch_s",
    "res_s",
    "h2_s",
    "coef_s",
    "gml_s",
    "mlp_s",
    "gh2_s",
    "gm_s",
    "col_s",
)


def named_call(kernel, refs):
    wanted = kernel.__code__.co_varnames[: kernel.__code__.co_argcount]
    kernel(*[refs[name] for name in wanted])


def forward_kernel(fast, *refs):
    names = FWD_IN + FWD_OUT
    names += FWD_FAST + FWD_TEMP + FWD_SUMS if fast else FWD_SUMS + FWD_TEMP
    refs = dict(zip(names, refs, strict=True))
    named_call(forward_row, refs)
    if fast:

        @pl.when(pl.program_id(0) == pl.num_programs(0) - 1)
        def _():
            named_call(forward_flush, refs)

        named_call(forward_mod, refs)


def forward_row(
    place,
    tok_own,
    tok_in,
    cot_own,
    cot_in,
    row,
    mod,
    head_tab,
    chan_tab,
    w_qkv,
    b_qv,
    w_proj,
    b_proj,
    w_fc1,
    b_fc1,
    w_fc2,
    b_fc2,
    w_router,
    out_own,
    out_far,
    hid_out,
    q_out,
    k_out,
    v_out,
    prob_out,
    gheads_out,
    gres_out,
    dwp,
    gmod,
    dw1,
    dw2,
    db2,
    dwr,
    x_s,
    cot_s,
    bias_s,
    hot_s,
    tab_s,
    mix_s,
    att_s,
    branch_s,
    res_s,
    h2_s,
    coef_s,
    gml_s,
    mlp_s,
    gh2_s,
    gm_s,
    col_s,
):
    length = x_s.shape[0]
    local = tok_own.shape[1]
    far = tok_in.shape[0]

    @pl.when(pl.program_id(0) == 0)
    def _():
        for ref in (dw1, dw2, dwp, db2, dwr):
            ref[...] = jnp.zeros_like(ref)
        for ref in (att_s, h2_s):
            ref[:, D:] = jnp.ones((length, LANES), BF16)

    x_s[0:local] = tok_own[0].astype(F32)
    cot_s[0:local] = cot_own[0].astype(F32)
    for j in range(far):
        x_s[(j + 1) * local : (j + 2) * local] = tok_in[j, 0].astype(F32)
        cot_s[(j + 1) * local : (j + 2) * local] = cot_in[j, 0].astype(F32)
    tab_s[...] = three_terms(mod[0])
    mlp_s[...] = jnp.zeros_like(mlp_s)
    gh2_s[...] = jnp.zeros_like(gh2_s)
    gm_s[...] = jnp.zeros_like(gm_s)
    id_row = row[0, 0:1, :]
    col_s[...] = row[0].T

    def first(i, _):
        part = pl.ds(i * TOK, TOK)
        hot = crop_rows(col_s[part, 1:2], TOK)
        hot_s[part] = hot
        bias_s[part] = jnp.where(col_s[part, 0:1] == id_row, 0.0, NEGATIVE)
        normal, _ = normalise(x_s[part])
        hidden = (normal * (1.0 + dot(hot, tab_s[:, D : 2 * D])) + dot(hot, tab_s[:, 0:D])).astype(
            BF16
        )
        hid_out[0, part] = hidden
        q_out[0, part] = (dot(hidden, w_qkv[:, 0:D]) + b_qv[:, 0:D]).astype(BF16) * BF16(
            HEAD_DIM**-0.5
        )
        k_out[0, part] = dot(hidden, w_qkv[:, D : 2 * D]).astype(BF16)
        v_out[0, part] = (dot(hidden, w_qkv[:, 2 * D :]) + b_qv[:, D:]).astype(BF16)
        return 0

    lax.fori_loop(0, length // TOK, first, 0)

    def attend(hp, _):
        lanes = pl.ds(pl.multiple_of(hp * PAIR, PAIR), PAIR)
        query, key = q_out[0, :, lanes], k_out[0, :, lanes]
        value_t = v_out[0, :, lanes].T
        for half in range(2):
            key_half = half_lanes(key, half)
            for c in range(length // TOK):
                cols = slice(c * TOK, (c + 1) * TOK)
                scores = dot_nt(key_half, query[cols]) + bias_s[:, cols]
                top = jnp.max(scores, 0, keepdims=True)
                numerator = jnp.exp(scores - top)
                scale = 1.0 / jnp.sum(numerator, 0, keepdims=True)
                prob = (numerator * scale).astype(BF16)
                prob_out[0, 2 * hp + half, :, cols] = prob
                mix_s[half * HEAD_DIM : (half + 1) * HEAD_DIM, cols] = dot(
                    value_t[half * HEAD_DIM : (half + 1) * HEAD_DIM], prob
                )
        keep_heads = dot(hot_s[...], head_tab[0, :, lanes])
        att_s[:, lanes] = (mix_s[...].T * keep_heads).astype(BF16)
        return 0

    lax.fori_loop(0, D // PAIR, attend, 0)

    def middle(i, _):
        part = pl.ds(i * TOK, TOK)
        hot = hot_s[part]
        live = jnp.where(col_s[part, 0:1] >= 0.0, 1.0, 0.0)
        branch = dot(att_s[part, 0:D], w_proj[...]) + b_proj[...]
        branch_s[part] = branch
        residual = x_s[part] + live * dot(hot, tab_s[:, 2 * D : 3 * D]) * branch
        res_s[part] = residual
        normal, _ = normalise(residual)
        hidden = (
            normal * (1.0 + dot(hot, tab_s[:, 4 * D : 5 * D])) + dot(hot, tab_s[:, 3 * D : 4 * D])
        ).astype(BF16)
        h2_s[part, 0:D] = hidden
        logit = jnp.sum(hidden.astype(F32) * w_router[...], -1, keepdims=True)
        rate = 1.0 / (1.0 + jnp.exp(-logit))
        keep = live * col_s[part, 2:3]
        coef = keep * rate
        coef_s[part, 0:1] = coef
        coef_s[part, 1:2] = coef * (1.0 - rate)
        gml = (cot_s[part] * coef * dot(hot, tab_s[:, 5 * D : 6 * D])).astype(BF16)
        gml_s[part] = gml
        db2[...] += dot_tn(gml, jnp.ones((TOK, LANES), BF16))
        return 0

    lax.fori_loop(0, length // TOK, middle, 0)

    def feed(c, _):
        units = pl.ds(pl.multiple_of(c * FCH, FCH), FCH)
        hidden, gml = h2_s[...], gml_s[...]
        pre = dot(hidden[:, 0:D], w_fc1[:, units]) + b_fc1[:, units]
        mask = dot(hot_s[...], chan_tab[0, :, units])
        square = pre * pre
        tanh = jnp.tanh(pre * (GELU_A + (GELU_A * GELU_B) * square))
        half = 0.5 * pre
        side = 0.5 + 0.5 * tanh
        act = (pre * side * mask).astype(BF16)
        slope = side + half * (1.0 - tanh * tanh) * (GELU_A + (3.0 * GELU_A * GELU_B) * square)
        mlp_s[...] += dot(act, w_fc2[units, :])
        dw2[units, :] += dot_tn(act, gml)
        gpre = (slope * mask * dot_nt(gml, w_fc2[units, :])).astype(BF16)
        dw1[units, :] += dot_tn(gpre, hidden)
        gh2_s[...] += dot_nt(gpre, w_fc1[:, units])
        return 0

    lax.fori_loop(0, FF // FCH, feed, 0)

    def last(i, _):
        part = pl.ds(i * TOK, TOK)
        hot = hot_s[part]
        live = jnp.where(col_s[part, 0:1] >= 0.0, 1.0, 0.0)
        coef = coef_s[part, 0:1]
        cot = cot_s[part]
        mlp = mlp_s[part] + b_fc2[...]
        gate2 = dot(hot, tab_s[:, 5 * D : 6 * D])
        residual = res_s[part]
        outcome = (residual + coef * gate2 * mlp).astype(BF16)
        mlp_s[part] = outcome.astype(F32)
        cot_mlp = cot * mlp
        grad_logit = jnp.sum(cot_mlp * gate2, -1, keepdims=True) * coef_s[part, 1:2]
        logit_high = grad_logit.astype(BF16).astype(F32)
        lane = lax.broadcasted_iota(jnp.int32, (TOK, LANES), 1)
        logit_terms = jnp.where(lane < LANES // 2, logit_high, grad_logit - logit_high)
        dwr[...] += dot_tn(h2_s[part, 0:D], logit_terms.astype(BF16))
        grad_hidden = gh2_s[part] + grad_logit * w_router[...]
        normal, inverse = normalise(residual)
        grad_res = cot + normalise_back(
            grad_hidden * (1.0 + dot(hot, tab_s[:, 4 * D : 5 * D])), normal, inverse
        )
        gres_out[0, part] = grad_res
        grad_live = grad_res * live
        grad_branch = (grad_live * dot(hot, tab_s[:, 2 * D : 3 * D])).astype(BF16)
        hot_t = crop_columns(row[0, 1:2, part], TOK)
        gm_s[:, 0:D] += dot(hot_t, (grad_live * branch_s[part]).astype(BF16))
        gm_s[:, D : 2 * D] += dot(hot_t, grad_hidden.astype(BF16))
        gm_s[:, 2 * D : 3 * D] += dot(hot_t, (grad_hidden * normal).astype(BF16))
        gm_s[:, 3 * D : 4 * D] += dot(hot_t, (cot_mlp * coef).astype(BF16))
        dwp[...] += dot_tn(grad_branch, att_s[part])
        gheads_out[0, part] = (
            dot_nt(grad_branch, w_proj[...]).astype(BF16).astype(F32) * dot(hot, head_tab[0])
        ).astype(BF16)
        return 0

    lax.fori_loop(0, length // TOK, last, 0)
    out_own[0] = mlp_s[0:local].astype(BF16)
    for j in range(far):
        out_far[j, 0] = mlp_s[(j + 1) * local : (j + 2) * local].astype(BF16)
    gmod[0] = gm_s[0:CROPS]


def lane_put(lane, column):
    position = lax.broadcasted_iota(jnp.int32, (column.shape[0], LANES), 1)
    return jnp.where(position == lane, column, 0.0)


def slot_of(near, inner, outer):
    return (near & (inner - 1)) * outer + near // inner


def forward_flush(place, dw1, dw2, dwp, db2, dwr, e_own, e_send, parcel):
    buckets, units, _ = e_own.shape
    depth = parcel.shape[1]

    def one(b, _):
        slot = slot_of(b ^ place[1], INNER, buckets // INNER)
        rows = pl.ds(pl.multiple_of(b * units, 8), units)
        first, second = dw1[rows, 0:D], dw2[rows, :]
        swap = place[0] == 0
        e_own[slot] = jnp.where(swap, first, second)
        e_send[slot] = jnp.where(swap, second, first).astype(BF16)
        held = jnp.zeros((depth, LANES), F32)
        for i in range(units // depth):
            held += lane_put(
                i, dw1[pl.ds(pl.multiple_of(b * units + i * depth, 8), depth), D : D + 1]
            )
        part = pl.ds(pl.multiple_of(b * depth, 8), depth)
        count = units // depth
        held += lane_put(count, db2[part, 0:1])
        held += lane_put(count + 1, dwp[part, D : D + 1])
        held += lane_put(count + 2, dwr[part, 0:1] + dwr[part, LANES // 2 : LANES // 2 + 1])
        parcel[slot] = held
        return 0

    lax.fori_loop(0, buckets, one, 0)


def forward_mod(place, gm_s, gme_own, gme_send):
    first, second = gm_s[0:CROPS, 0:D], gm_s[0:CROPS, D : 2 * D]
    swap = place[0] == 0
    gme_own[0] = jnp.where(swap, first, second)
    gme_send[0] = jnp.where(swap, second, first)


BWD_IN = (
    "place",
    "tok_own",
    "tok_in",
    "row",
    "mod",
    "w_qkv",
    "hid",
    "q_in",
    "k_in",
    "v_in",
    "prob_in",
    "gheads",
    "gres",
)
BWD_FAST_IN = ("dwp", "parcel_in", "gm_in")
BWD_OUT = ("gt_own", "gt_far")
BWD_FAST = ("l_own", "l_send", "parcel", "gml_own", "gml_send")
BWD_TEMP = ("gp_s", "dk_s", "dv_s", "dq_s", "x_s", "tab_s", "hid_s", "gm_s", "col_s")


def backward_kernel(fast, *refs):
    names = BWD_IN
    if fast:
        names += BWD_FAST_IN + BWD_OUT + BWD_FAST + BWD_TEMP + ("dwq",)
    else:
        names += BWD_OUT + ("dwq", "gmod") + BWD_TEMP
    refs = dict(zip(names, refs, strict=True))
    named_call(backward_row, refs)
    if not fast:
        refs["gmod"][0] = refs["gm_s"][0:CROPS]
        return

    @pl.when(pl.program_id(0) == pl.num_programs(0) - 1)
    def _():
        named_call(backward_flush, refs)

    named_call(backward_mod, refs)


def backward_mod(place, gm_s, gm_in, gml_own, gml_send):
    first, second = gm_s[0:CROPS], gm_in[0, :, 2 * D :]
    swap = place[0] == 0
    gml_own[0] = jnp.where(swap, first, second)
    gml_send[0] = jnp.where(swap, second, first)


def backward_flush(place, dwq, dwp, parcel_in, l_own, l_send, parcel):
    buckets, lines, _ = l_own.shape
    depth = parcel.shape[1]

    def one(b, _):
        slot = slot_of(b ^ place[1], INNER, buckets // INNER)
        start = b * 3 * depth
        first = dwq[pl.ds(pl.multiple_of(start, 8), lines), 0:D]
        second = jnp.concatenate(
            [
                dwq[pl.ds(pl.multiple_of(start + lines, 8), 3 * depth - lines), 0:D],
                dwp[pl.ds(pl.multiple_of(b * depth, 8), depth), 0:D],
            ],
            0,
        )
        swap = place[0] == 0
        l_own[slot] = jnp.where(swap, first, second)
        l_send[slot] = jnp.where(swap, second, first).astype(BF16)
        held = parcel_in[slot]
        start = b * 2 * depth
        start = jnp.where(start < D, start, start + D)
        for i in range(2):
            held += lane_put(
                7 + i, dwq[pl.ds(pl.multiple_of(start + i * depth, 8), depth), D : D + 1]
            )
        parcel[slot] = held
        return 0

    lax.fori_loop(0, buckets, one, 0)


def backward_row(
    place,
    tok_own,
    tok_in,
    row,
    mod,
    w_qkv,
    hid,
    q_in,
    k_in,
    v_in,
    prob_in,
    gheads,
    gres,
    gt_own,
    gt_far,
    dwq,
    gp_s,
    dk_s,
    dv_s,
    dq_s,
    x_s,
    tab_s,
    hid_s,
    gm_s,
    col_s,
):
    length = x_s.shape[0]
    local = tok_own.shape[1]
    far = tok_in.shape[0]

    @pl.when(pl.program_id(0) == 0)
    def _():
        dwq[...] = jnp.zeros_like(dwq)
        hid_s[:, D:] = jnp.ones((length, LANES), BF16)

    x_s[0:local] = tok_own[0].astype(F32)
    for j in range(far):
        x_s[(j + 1) * local : (j + 2) * local] = tok_in[j, 0].astype(F32)
    tab_s[...] = three_terms(mod[0, :, D : 2 * D])
    col_s[...] = row[0].T
    gm_s[...] = jnp.zeros_like(gm_s)

    def attend(hp, _):
        lanes = pl.ds(pl.multiple_of(hp * PAIR, PAIR), PAIR)
        query, key, value = q_in[0, :, lanes], k_in[0, :, lanes], v_in[0, :, lanes]
        grad = gheads[0, :, lanes]
        key_t = key.T
        dk_s[...] = jnp.zeros_like(dk_s)
        dv_s[...] = jnp.zeros_like(dv_s)
        for half in range(2):
            value_half = half_lanes(value, half)
            for c in range(length // TOK):
                cols = slice(c * TOK, (c + 1) * TOK)
                prob_low = prob_in[0, 2 * hp + half, :, cols]
                prob = prob_low.astype(F32)
                grad_cols = grad[cols]
                product = prob * dot_nt(value_half, grad_cols)
                inner = jnp.sum(product, 0, keepdims=True)
                grad_scores = (product - prob * inner).astype(BF16)
                dv_s[...] += dot(prob_low, half_lanes(grad_cols, half))
                dk_s[...] += dot(grad_scores, half_lanes(query[cols], half))
                dq_s[half * HEAD_DIM : (half + 1) * HEAD_DIM, cols] = dot(
                    key_t[half * HEAD_DIM : (half + 1) * HEAD_DIM], grad_scores
                )
        gp_s[:, lanes] = (dq_s[...].T * HEAD_DIM**-0.5).astype(BF16)
        gp_s[:, pl.ds(pl.multiple_of(D + hp * PAIR, PAIR), PAIR)] = dk_s[...].astype(BF16)
        gp_s[:, pl.ds(pl.multiple_of(2 * D + hp * PAIR, PAIR), PAIR)] = dv_s[...].astype(BF16)
        return 0

    lax.fori_loop(0, D // PAIR, attend, 0)

    def last(i, _):
        part = pl.ds(i * TOK, TOK)
        hot = crop_rows(col_s[part, 1:2], TOK)
        grad = gp_s[part]
        grad_hidden = dot_nt(grad, w_qkv[...])
        normal, inverse = normalise(x_s[part])
        hot_t = crop_columns(row[0, 1:2, part], TOK)
        gm_s[:, 0:D] += dot(hot_t, grad_hidden.astype(BF16))
        gm_s[:, D : 2 * D] += dot(hot_t, (grad_hidden * normal).astype(BF16))
        x_s[part] = gres[0, part] + normalise_back(
            grad_hidden * (1.0 + dot(hot, tab_s[...])), normal, inverse
        )
        return 0

    lax.fori_loop(0, length // TOK, last, 0)
    hid_s[:, 0:D] = hid[0]
    for c in range(3):
        rows = slice(c * D, (c + 1) * D)
        dwq[rows, :] += dot_tn(gp_s[:, rows], hid_s[...])
    gt_own[0] = x_s[0:local].astype(BF16)
    for j in range(far):
        gt_far[j, 0] = x_s[(j + 1) * local : (j + 2) * local].astype(BF16)


def seq_order(place, own, far):
    own, far = own.reshape(-1, own.shape[-1]), far.reshape(-1, far.shape[-1])
    return jnp.where(
        place[0] == 0, jnp.concatenate([own, far], 0), jnp.concatenate([far, own], 0)
    ).astype(BF16)


def early_pack(place, e_own, e_in, gm_own, gm_in, silu, keep, *sends):
    outer = keep.shape[0]
    depth = D // e_own.shape[0]
    ada = dot_tn(silu[...], seq_order(place, gm_own[...], gm_in[...]))
    for slot in range(e_own.shape[0]):
        total = jnp.concatenate(
            [e_own[slot] + e_in[slot].astype(F32), ada[slot * depth : (slot + 1) * depth]], 0
        )
        if slot < outer:
            keep[slot] = total
        else:
            sends[slot // outer - 1][slot % outer] = total.astype(BF16)


def early_line(own, in1, in2, in3, keep, *sends):
    for k in range(own.shape[0]):
        total = own[k] + in1[k].astype(F32) + in2[k].astype(F32) + in3[k].astype(F32)
        if k == 0:
            keep[...] = total
        else:
            sends[k - 1][...] = total.astype(BF16)


def late_pack(
    place,
    l_own,
    l_in,
    gml_own,
    gml_in,
    gme_own,
    gme_in,
    silu,
    ada,
    slope,
    ids,
    parcel,
    keep,
    s1,
    s2,
    s3,
    gm_s,
    ada_s,
):
    sends = (s1, s2, s3)
    outer = keep.shape[0]
    buckets, lines, _ = l_own.shape
    depth = D // buckets
    crops = silu.shape[0]
    late = seq_order(place, gml_own[...], gml_in[...])
    early = seq_order(place, gme_own[...], gme_in[...])
    gm_s[...] = jnp.zeros_like(gm_s)

    @pl.when(place[0] == 0)
    def _():
        gm_s[crops : 2 * crops, 0 : 2 * D] = late
        gm_s[crops : 2 * crops, 2 * D :] = early

    @pl.when(place[0] != 0)
    def _():
        gm_s[crops : 2 * crops, 0:D] = early
        gm_s[crops : 2 * crops, D:] = late

    grads = dot_tn(silu[...], late)
    crop_t = dot_nt(ada[...], gm_s[...]) * slope[...]
    ada_s[...] = dot_tn(gm_s[...], jnp.ones((LANES, LANES), BF16))
    for slot in range(buckets):
        bucket = place[1] ^ ((slot // outer) + INNER * (slot % outer))
        held = parcel[slot] + crop_t[slot * depth : (slot + 1) * depth] + ids[...]
        for i in range(3):
            start = pl.multiple_of(bucket * 3 * depth + i * depth, 8)
            held += lane_put(9 + i, ada_s[pl.ds(start, depth), 0:1])
        part = slice(slot * depth, (slot + 1) * depth)
        total = jnp.concatenate(
            [
                l_own[slot] + l_in[slot].astype(F32),
                grads[part, 0:D],
                grads[part, D:],
                jnp.concatenate([held[8 * i : 8 * (i + 1)] for i in range(3)], 1),
            ],
            0,
        )
        if slot < outer:
            keep[slot] = total
        else:
            sends[slot // outer - 1][slot % outer] = total.astype(BF16)


def late_line(own, in1, in2, in3, keep, *sends):
    sums = own.shape[1] - 8
    for k in range(own.shape[0]):
        pieces = [own[k]] + [piece[k].astype(F32) for piece in (in1, in2, in3)]
        total = pieces[0][0:sums]
        for piece in pieces[1:]:
            total = total + piece[0:sums]
        total = jnp.concatenate([total] + [piece[sums:] for piece in pieces], 0)
        if k == 0:
            keep[...] = total
        else:
            sends[k - 1][...] = total.astype(BF16)


def last_pack(place, early, e1, e2, e3, late, l1, l2, l3, parts, ada):
    depth = ada.shape[0]
    units = early.shape[0] - depth
    e_sum = early[...] + e1[...].astype(F32) + e2[...].astype(F32) + e3[...].astype(F32)
    pieces = [late[...]] + [piece[...].astype(F32) for piece in (l1, l2, l3)]
    sums = late.shape[0] - 8 * INNER
    lines = sums - 2 * depth
    l_sum = pieces[0][0:sums]
    for piece in pieces[1:]:
        l_sum = l_sum + piece[0:sums]
    parts[0:units] = e_sum[0:units]
    parts[units : units + lines] = l_sum[0:lines]
    for i, piece in enumerate(pieces):
        start = units + lines + 8 * INNER * i
        parts[start : start + 8 * INNER] = piece[sums:]
    tail, first, second = e_sum[units:], l_sum[lines : lines + depth], l_sum[lines + depth :]
    swap = place[0] == 0
    ada[:, 0:D] = jnp.where(swap, first, tail)
    ada[:, D : 2 * D] = jnp.where(swap, second, first)
    ada[:, 2 * D :] = jnp.where(swap, tail, second)


def spread(columns, depth):
    line = lax.broadcasted_iota(jnp.int32, (depth, LANES), 0)
    lane = lax.broadcasted_iota(jnp.int32, (depth, LANES), 1)
    total = jnp.zeros((depth, LANES), F32)
    for i, column in enumerate(columns):
        total += jnp.where(lane - depth * i == line, column, 0.0)
    return jnp.sum(total, 0, keepdims=True)


def finish(
    place, own, far, table, qkv, qv, proj, bp, fc1, b1, fc2, b2, router, b_ada, crop_s, hot_s
):
    units, depth = fc2.shape[0], router.shape[1]
    lines = 4 * depth // 2
    swap = place[0] == 0
    own_e, far_e = own[0:units], far[0:units]
    fc1[...] = jnp.where(swap, own_e, far_e)
    fc2[...] = jnp.where(swap, far_e, own_e)
    own_l, far_l = own[units : units + lines], far[units : units + lines]
    first, second = jnp.where(swap, own_l, far_l), jnp.where(swap, far_l, own_l)
    cut = 3 * depth - lines
    qkv[...] = jnp.concatenate([first, second[0:cut]], 0)
    proj[...] = second[cut:]
    own_sum = jnp.zeros((depth, LANES), F32)
    far_sum = jnp.zeros((depth, LANES), F32)
    sources = (own.shape[0] - units - lines) // 8
    wide = lax.broadcasted_iota(jnp.int32, (32, hot_s.shape[1]), 1).astype(F32)
    for source in range(sources):
        rows = slice(units + lines + 8 * source, units + lines + 8 * (source + 1))
        own_p = jnp.concatenate([own[rows, i * LANES : (i + 1) * LANES] for i in range(3)], 0)
        far_p = jnp.concatenate([far[rows, i * LANES : (i + 1) * LANES] for i in range(3)], 0)
        own_sum += own_p
        far_sum += far_p
        both = (own_p + far_p).T
        grads = both[32:64]
        high = grads.astype(BF16).astype(F32)
        crops = slice(32 * source, 32 * (source + 1))
        crop_s[crops, 0:depth] = high
        crop_s[crops, 32 : 32 + depth] = grads - high
        ids = own_p.T
        crop_id = ids[64:96, 0:1] * 8.0 + ids[96:128, 0:1]
        hot_s[crops] = jnp.where(crop_id == wide, 1.0, 0.0).astype(BF16)
    terms = dot_tn(crop_s[:, 0:64].astype(BF16), hot_s[...])
    table[...] = (terms[0:depth] + terms[32 : 32 + depth])[:, 0 : table.shape[1]]
    total = own_sum + far_sum

    def lane(values, i):
        return values[:, i : i + 1]

    b1[...] = spread([lane(total, i) for i in range(4)], depth)[:, 0:units]
    b2[...] = spread([lane(total, 4)], depth)[:, 0:depth]
    bp[...] = spread([lane(total, 5)], depth)[:, 0:depth]
    router[...] = spread([lane(total, 6)], depth)[:, 0:depth]
    qv[...] = spread([lane(total, 7), lane(total, 8)], depth)[:, 0 : 2 * depth]
    b_ada[...] = spread([lane(own_sum, 9 + i) for i in range(3)], depth)[:, 0 : 3 * depth]


def whole(shape):
    return pl.BlockSpec(shape, lambda r, place: (0,) * len(shape))


def per_row(shape):
    return pl.BlockSpec((1,) + shape, lambda r, place: (r,) + (0,) * len(shape))


def per_far(count, shape):
    return pl.BlockSpec((count, 1) + shape, lambda r, place: (0, r) + (0,) * len(shape))


def body(
    tokens,
    cotangent,
    segment_ids,
    pad_counts,
    timesteps,
    classes,
    head_mask,
    channel_mask,
    keep_mask,
    class_table,
    w_ada,
    b_ada,
    w_qkv,
    bias_qv,
    w_proj,
    b_proj,
    w_fc1,
    b_fc1,
    w_fc2,
    b_fc2,
    w_router,
):
    seqs, buckets = lax.axis_size("seq"), lax.axis_size("bucket")
    me_s, me_b = lax.axis_index("seq"), lax.axis_index("bucket")
    row_count, local, _ = tokens.shape
    mine = row_count // seqs
    length = local * seqs
    crops_here = row_count * CROPS
    crops_mine = mine * CROPS
    inner, outer = 4, buckets // 4

    def seq_hop(value, step):
        return lax.ppermute(value, "seq", [(i, i ^ step) for i in range(seqs)])

    def plane_hop(value, step):
        return lax.ppermute(value, "bucket", [(i, i ^ step) for i in range(buckets)])

    def line_hop(value, step):
        return lax.ppermute(value, "bucket", [(i, i ^ (step * inner)) for i in range(buckets)])

    def slab(value, device, count):
        return lax.dynamic_slice_in_dim(value, device * count, count, 0)

    def by_device(pieces, device):
        chosen = pieces[0]
        for j in range(1, seqs):
            chosen = jnp.where((me_s ^ device) == j, pieces[j], chosen)
        return chosen

    def deal_rows(value):
        return [seq_hop(slab(value, me_s ^ j, mine), j) for j in range(1, seqs)]

    tok_in = jnp.stack(deal_rows(tokens))
    cot_in = jnp.stack(deal_rows(cotangent))
    keep_in = deal_rows(keep_mask)

    ada_parts = [w_ada] + [line_hop(w_ada, k) for k in range(1, outer)]
    ada_line = jnp.concatenate(ada_parts, 0)
    ada_all = jnp.concatenate([ada_line] + [plane_hop(ada_line, k) for k in range(1, inner)], 0)

    position = jnp.arange(length, dtype=jnp.int32)
    live_row = position[None, :] < (length - pad_counts)[:, None]
    attend_ids = jnp.where(live_row, segment_ids, -1)
    both = jnp.stack([segment_ids, attend_ids]).astype(F32)
    both = lax.dynamic_slice_in_dim(both, me_s * mine, mine, 1)
    both = jnp.concatenate(
        [lax.dynamic_slice_in_dim(both, (me_s ^ j) * local, local, 2) for j in range(seqs)], 2
    )
    keep_all = jnp.concatenate([slab(keep_mask, me_s, mine)] + keep_in, 1).astype(F32)
    row = jnp.stack([both[1], both[0], keep_all, keep_all], 1)

    half_width = D // 2
    frequency = jnp.exp(-math.log(10000.0) * jnp.arange(half_width, dtype=F32) / half_width)
    angles = timesteps.reshape(crops_here, 1).astype(F32) * frequency
    class_ids = classes.reshape(crops_here)
    class_hot = (class_ids[:, None] == jnp.arange(NCLASS, dtype=jnp.int32)).astype(BF16)
    condition = jnp.concatenate([jnp.cos(angles), jnp.sin(angles)], -1) + dot(
        class_hot, class_table
    )
    sigmoid = 1.0 / (1.0 + jnp.exp(-condition))
    silu_low = (condition * sigmoid).astype(BF16)
    silu_slope = sigmoid * (1.0 + condition * (1.0 - sigmoid))
    near = jnp.arange(buckets)
    order = me_b ^ ((near // outer) + inner * (near % outer))
    depth = D // buckets
    silu_near = jnp.take(silu_low.reshape(crops_here, buckets, depth), order, axis=1).reshape(
        crops_here, D
    )
    slope_near = jnp.take(silu_slope.reshape(crops_here, buckets, depth), order, axis=1).reshape(
        crops_here, D
    )
    mod_part = dot(silu_near, ada_all) + b_ada.astype(F32)
    mod_pieces = [slab(mod_part, me_s, crops_mine)] + deal_rows_of(mod_part, seqs, me_s, crops_mine)
    modulation = jnp.concatenate([by_device(mod_pieces, d) for d in range(seqs)], 1).reshape(
        mine, CROPS, 6 * D
    )

    def table_of(mask, width):
        wide = jnp.repeat(mask, width, axis=-1).astype(BF16)
        return jnp.pad(wide, ((0, 0), (0, 3 * CROPS), (0, 0)))

    head_tab = table_of(slab(head_mask, me_s, mine), HEAD_DIM)
    chan_tab = table_of(slab(channel_mask, me_s, mine), FF // CGROUPS)
    place = jnp.stack([me_s, me_b]).astype(jnp.int32)
    own = pl.BlockSpec((1, local, D), lambda r, place: (place[0] * mine + r, 0, 0))
    far = seqs - 1
    bias_row = bias_qv.astype(F32).reshape(1, 2 * D)

    def struct(shape, kind=F32):
        return jax.ShapeDtypeStruct(shape, kind)

    lanes = LANES
    fast = (
        seqs == 2 and buckets == 16 and crops_here == 4 * CROPS and (FF // buckets) % (4 * depth) == 0
    )
    if fast:
        slope_t = jnp.pad(slope_near.T, ((0, 0), (crops_here, lanes - 2 * crops_here)))
        id_lanes = jnp.pad(
            jnp.concatenate([class_ids // 8, class_ids % 8]).astype(F32)[None],
            ((0, depth - 1), (lanes - 2 * crops_here, 0)),
        )
    sum_shapes = [(FF, D + lanes), (FF, D), (D, lanes), (D, lanes)]
    out_names = [
        (struct((mine, local, D), BF16), per_row((local, D))),
        (struct((far, mine, local, D), BF16), per_far(far, (local, D))),
    ]
    out_names += [(struct((mine, length, D), BF16), per_row((length, D)))] * 4
    out_names += [
        (struct((mine, HEADS, length, length), BF16), per_row((HEADS, length, length))),
        (struct((mine, length, D), BF16), per_row((length, D))),
        (struct((mine, length, D)), per_row((length, D))),
        (struct((D, D + lanes)), whole((D, D + lanes))),
        (struct((mine, CROPS, 4 * D)), per_row((CROPS, 4 * D))),
    ]
    if fast:
        units = FF // buckets
        out_names += [
            (struct((buckets, units, D)), whole((buckets, units, D))),
            (struct((buckets, units, D), BF16), whole((buckets, units, D))),
            (struct((buckets, depth, lanes)), whole((buckets, depth, lanes))),
            (struct((mine, CROPS, D)), per_row((CROPS, D))),
            (struct((mine, CROPS, D)), per_row((CROPS, D))),
        ]
    else:
        out_names += [(struct(shape), whole(shape)) for shape in sum_shapes]
    scratch = [
        pltpu.VMEM((length, D), F32),
        pltpu.VMEM((length, D), F32),
        pltpu.VMEM((length, length), F32),
        pltpu.VMEM((length, 4 * CROPS), BF16),
        pltpu.VMEM((4 * CROPS, 6 * D), BF16),
        pltpu.VMEM((PAIR, length), F32),
        pltpu.VMEM((length, D + lanes), BF16),
        pltpu.VMEM((length, D), F32),
        pltpu.VMEM((length, D), F32),
        pltpu.VMEM((length, D + lanes), BF16),
        pltpu.VMEM((length, 2), F32),
        pltpu.VMEM((length, D), BF16),
        pltpu.VMEM((length, D), F32),
        pltpu.VMEM((length, D), F32),
        pltpu.VMEM((2 * CROPS, 4 * D), F32),
        pltpu.VMEM((length, 4), F32),
    ]
    if fast:
        scratch += [pltpu.VMEM(shape, F32) for shape in sum_shapes]
    tokens_here = mine * length
    (
        out_own,
        out_far,
        hid,
        query,
        key,
        value,
        prob,
        grad_heads,
        grad_res,
        dwp,
        gmod_late,
        *sums,
    ) = pl.pallas_call(
        partial(forward_kernel, fast),
        name="layer_forward",
        grid_spec=pltpu.PrefetchScalarGridSpec(
            num_scalar_prefetch=1,
            grid=(mine,),
            in_specs=[
                own,
                per_far(far, (local, D)),
                own,
                per_far(far, (local, D)),
                per_row((4, length)),
                per_row((CROPS, 6 * D)),
                per_row((4 * CROPS, D)),
                per_row((4 * CROPS, FF)),
                whole((D, 3 * D)),
                whole((1, 2 * D)),
                whole((D, D)),
                whole((1, D)),
                whole((D, FF)),
                whole((1, FF)),
                whole((FF, D)),
                whole((1, D)),
                whole((1, D)),
            ],
            out_specs=[spec for _, spec in out_names],
            scratch_shapes=scratch,
        ),
        out_shape=[shape for shape, _ in out_names],
        cost_estimate=pl.CostEstimate(
            flops=2 * tokens_here * (4 * D * D + 6 * D * FF + 2 * D * length),
            transcendentals=tokens_here * (FF + HEADS * length),
            bytes_accessed=20_000_000,
        ),
    )(
        place,
        tokens,
        tok_in,
        cotangent,
        cot_in,
        row,
        modulation,
        head_tab,
        chan_tab,
        w_qkv,
        bias_row,
        w_proj,
        b_proj.astype(F32).reshape(1, D),
        w_fc1,
        b_fc1.astype(F32).reshape(1, FF),
        w_fc2,
        b_fc2.astype(F32).reshape(1, D),
        w_router.astype(F32).reshape(1, D),
    )

    def return_rows(own_piece, far_pieces):
        pieces = [own_piece] + [seq_hop(far_pieces[j - 1], j) for j in range(1, seqs)]
        return jnp.concatenate([by_device(pieces, d) for d in range(seqs)], 0)

    def sum_over_all(parts):
        joined = jnp.concatenate([part.reshape(buckets, -1, D) for part in parts], 1)
        lines = joined.shape[1] // seqs
        joined = joined.reshape(buckets, seqs, lines, D)
        joined = jnp.take(joined, order, axis=0)
        total = lax.dynamic_index_in_dim(joined, me_s, 1, keepdims=False)
        for j in range(1, seqs):
            sent = lax.dynamic_index_in_dim(joined, me_s ^ j, 1, keepdims=False).astype(BF16)
            total = total + seq_hop(sent, j).astype(F32)
        total = sum_over_buckets(total)
        pieces = [total] + [seq_hop(total, j) for j in range(1, seqs)]
        return jnp.concatenate([by_device(pieces, d) for d in range(seqs)], 0)

    def sum_over_buckets(total):
        total = total.reshape((inner, outer) + total.shape[1:])
        plane = total[0]
        low = total.astype(BF16)
        for k in range(1, inner):
            plane = plane + plane_hop(low[k], k).astype(F32)
        line = plane[0]
        low = plane.astype(BF16)
        for k in range(1, outer):
            line = line + line_hop(low[k], k).astype(F32)
        return line

    output = return_rows(out_own, out_far)

    def glue(kernel, shapes, *operands, temps=()):
        return pl.pallas_call(
            kernel,
            name=kernel.__name__,
            in_specs=[pl.BlockSpec(memory_space=pltpu.SMEM)] * (operands[0] is place)
            + [pl.BlockSpec(memory_space=pltpu.VMEM)] * (len(operands) - (operands[0] is place)),
            out_specs=[pl.BlockSpec(memory_space=pltpu.VMEM)] * len(shapes),
            out_shape=shapes,
            scratch_shapes=list(temps),
            cost_estimate=pl.CostEstimate(flops=0, transcendentals=0, bytes_accessed=6_000_000),
        )(*operands)

    back_in = [
        (place, None),
        (tokens, own),
        (tok_in, per_far(far, (local, D))),
        (row, per_row((4, length))),
        (modulation, per_row((CROPS, 6 * D))),
        (w_qkv, whole((D, 3 * D))),
        (hid, per_row((length, D))),
        (query, per_row((length, D))),
        (key, per_row((length, D))),
        (value, per_row((length, D))),
        (prob, per_row((HEADS, length, length))),
        (grad_heads, per_row((length, D))),
        (grad_res, per_row((length, D))),
    ]
    back_out = [
        (struct((mine, local, D), BF16), per_row((local, D))),
        (struct((far, mine, local, D), BF16), per_far(far, (local, D))),
    ]
    back_temp = [
        pltpu.VMEM((length, 3 * D), BF16),
        pltpu.VMEM((length, PAIR), F32),
        pltpu.VMEM((length, PAIR), F32),
        pltpu.VMEM((PAIR, length), F32),
        pltpu.VMEM((length, D), F32),
        pltpu.VMEM((4 * CROPS, D), BF16),
        pltpu.VMEM((length, D + lanes), BF16),
        pltpu.VMEM((2 * CROPS, 2 * D), F32),
        pltpu.VMEM((length, 4), F32),
    ]
    if fast:
        lines = 2 * depth
        e_own, e_send, parcel, gme_own, gme_send = sums
        e_in, gme_in = seq_hop(e_send, 1), seq_hop(gme_send, 1)
        early = units + depth
        keep, *sends = glue(
            early_pack,
            [struct((outer, early, D))] + [struct((outer, early, D), BF16)] * 3,
            place,
            e_own,
            e_in,
            gme_own,
            gme_in,
            silu_near,
        )
        early_plane = [plane_hop(sends[k - 1], k) for k in range(1, inner)]
        prob, keep = lax.optimization_barrier((prob, keep))
        back_in[10] = (prob, back_in[10][1])
        back_in += [
            (dwp, whole((D, D + lanes))),
            (parcel, whole((buckets, depth, lanes))),
            (gmod_late, per_row((CROPS, 4 * D))),
        ]
        back_out += [
            (struct((buckets, lines, D)), whole((buckets, lines, D))),
            (struct((buckets, lines, D), BF16), whole((buckets, lines, D))),
            (struct((buckets, depth, lanes)), whole((buckets, depth, lanes))),
            (struct((mine, CROPS, 2 * D)), per_row((CROPS, 2 * D))),
            (struct((mine, CROPS, 2 * D)), per_row((CROPS, 2 * D))),
        ]
        back_temp.append(pltpu.VMEM((3 * D, D + lanes), F32))
    else:
        back_out += [
            (struct((3 * D, D + lanes)), whole((3 * D, D + lanes))),
            (struct((mine, CROPS, 2 * D)), per_row((CROPS, 2 * D))),
        ]
    gt_own, gt_far, *rest = pl.pallas_call(
        partial(backward_kernel, fast),
        name="layer_backward",
        grid_spec=pltpu.PrefetchScalarGridSpec(
            num_scalar_prefetch=1,
            grid=(mine,),
            in_specs=[spec for _, spec in back_in[1:]],
            out_specs=[spec for _, spec in back_out],
            scratch_shapes=back_temp,
        ),
        out_shape=[shape for shape, _ in back_out],
        cost_estimate=pl.CostEstimate(
            flops=2 * tokens_here * (6 * D * D + 5 * D * length),
            transcendentals=0,
            bytes_accessed=20_000_000,
        ),
    )(*[array for array, _ in back_in])
    if fast:
        early_plane, (gt_own, gt_far, *rest) = lax.optimization_barrier(
            (early_plane, (gt_own, gt_far, *rest))
        )
        l_own, l_send, parcel, gml_own, gml_send = rest
        l_in, gml_in = seq_hop(l_send, 1), seq_hop(gml_send, 1)
        late = lines + 2 * depth + 8
        late_keep, *late_sends = glue(
            late_pack,
            [struct((outer, late, D))] + [struct((outer, late, D), BF16)] * 3,
            place,
            l_own,
            l_in,
            gml_own,
            gml_in,
            gme_own,
            gme_in,
            silu_near,
            ada_all,
            slope_t,
            id_lanes,
            parcel,
            temps=[pltpu.VMEM((lanes, 3 * D), BF16), pltpu.VMEM((3 * D, lanes), F32)],
        )
        late_plane = [plane_hop(late_sends[k - 1], k) for k in range(1, inner)]
        keep, *sends = glue(
            early_line,
            [struct((early, D))] + [struct((early, D), BF16)] * 3,
            keep,
            *early_plane,
        )
        early_in = [line_hop(sends[k - 1], k) for k in range(1, outer)]
        late = late + 24
        late_keep, *late_sends = glue(
            late_line,
            [struct((late, D))] + [struct((late, D), BF16)] * 3,
            late_keep,
            *late_plane,
        )
        late_in = [line_hop(late_sends[k - 1], k) for k in range(1, outer)]
        grad_tokens = return_rows(gt_own, gt_far)
        parts, grad_w_ada = glue(
            last_pack,
            [struct((units + lines + 8 * buckets, D)), struct((depth, 3 * D))],
            place,
            keep,
            *early_in,
            late_keep,
            *late_in,
        )
        table, qkv, qv, proj, bp, fc1, b1, fc2, b2, router, v_ada = glue(
            finish,
            [
                struct((depth, NCLASS)),
                struct((3 * depth, D)),
                struct((1, 2 * depth)),
                struct((depth, D)),
                struct((1, depth)),
                struct((units, D)),
                struct((1, units)),
                struct((units, D)),
                struct((1, depth)),
                struct((1, depth)),
                struct((1, 3 * depth)),
            ],
            place,
            parts,
            seq_hop(parts, 1),
            temps=[
                pltpu.VMEM((buckets * crops_here, lanes), F32),
                pltpu.VMEM((buckets * crops_here, 8 * lanes), BF16),
            ],
        )
        return (
            output,
            grad_tokens,
            table.T,
            grad_w_ada,
            v_ada,
            qkv.T,
            qv.reshape(-1),
            proj.T,
            bp.reshape(-1),
            fc1.T,
            b1.reshape(-1),
            fc2,
            b2.reshape(-1),
            router.reshape(-1),
        )

    dw1, dw2, db2, dwr = sums
    dwq, gmod_first = rest
    early = sum_over_all([dw1[:, 0:D], dw2])
    grad_tokens = return_rows(gt_own, gt_far)
    late = sum_over_all([dwq[:, 0:D], dwp[:, 0:D]])

    grad_mod = jnp.concatenate([gmod_first, gmod_late], -1).astype(BF16).reshape(crops_mine, 6 * D)
    width = 6 * D // seqs
    mod_pieces = [lax.dynamic_slice_in_dim(grad_mod, me_s * width, width, 1)] + [
        seq_hop(lax.dynamic_slice_in_dim(grad_mod, (me_s ^ j) * width, width, 1), j)
        for j in range(1, seqs)
    ]
    grad_mod = jnp.concatenate([by_device(mod_pieces, d) for d in range(seqs)], 0)
    grad_w_ada = sum_over_buckets(
        lax.dot_general(
            silu_near, grad_mod, (((0,), (0,)), ((), ())), preferred_element_type=F32
        ).reshape(buckets, depth, width)
    )

    grad_b_ada = jnp.sum(grad_mod.astype(F32), 0).reshape(buckets, -1)
    grad_silu = dot_nt(grad_mod, ada_all)
    small = jnp.concatenate(
        [
            part.reshape(buckets, -1)
            for part in (
                dw1[:, D],
                db2[:, 0],
                dwp[:, D],
                dwr[:, 0] + dwr[:, lanes // 2],
                jnp.concatenate([dwq[0:D, D], dwq[2 * D :, D]]),
            )
        ],
        1,
    )
    small_size = small.shape[1]
    for j in [1 << b for b in range(seqs.bit_length() - 1)]:
        grad_silu = grad_silu + seq_hop(grad_silu, j)
        small = small + seq_hop(small, j)
    grad_condition = grad_silu * slope_near
    crop_part = grad_condition.reshape(crops_here, buckets, depth).swapaxes(0, 1)
    parcel = jnp.concatenate(
        [
            crop_part.reshape(buckets, crops_here * depth),
            jnp.take(small, order, axis=0),
            jnp.take(grad_b_ada, order, axis=0),
            jnp.broadcast_to(class_ids.astype(F32)[None], (buckets, crops_here)),
        ],
        1,
    ).reshape(inner, outer, -1)
    parcel = jnp.stack([parcel[0]] + [plane_hop(parcel[k], k) for k in range(1, inner)])
    parcel = jnp.stack([parcel[:, 0]] + [line_hop(parcel[:, k], k) for k in range(1, outer)])
    parcel = parcel.reshape(buckets, -1)
    first = crops_here * depth
    crop_grads = parcel[:, :first].reshape(buckets * crops_here, depth)
    small = jnp.sum(parcel[:, first : first + small_size + grad_b_ada.shape[1]], 0)
    source_ids = parcel[:, first + small_size + grad_b_ada.shape[1] :].reshape(1, -1)
    hot = (jnp.arange(NCLASS, dtype=F32)[:, None] == source_ids).astype(F32)
    grad_table = jnp.dot(hot, crop_grads, precision=lax.Precision.HIGHEST)

    ff_part, d_part = FF // buckets, D // buckets
    cuts = [0]
    for size in (ff_part, d_part, d_part, d_part, 2 * d_part, grad_b_ada.shape[1]):
        cuts.append(cuts[-1] + size)
    v_b1, v_b2, v_bp, v_wr, v_qv, v_ada = (small[a:b] for a, b in zip(cuts[:-1], cuts[1:]))
    return (
        output,
        grad_tokens,
        grad_table,
        grad_w_ada,
        v_ada.reshape(1, -1),
        late[: 3 * d_part].T,
        v_qv,
        late[3 * d_part :].T,
        v_bp,
        early[:ff_part].T,
        v_b1,
        early[ff_part:],
        v_b2,
        v_wr,
    )


def deal_rows_of(value, seqs, me_s, count):
    return [
        lax.ppermute(
            lax.dynamic_slice_in_dim(value, (me_s ^ j) * count, count, 0),
            "seq",
            [(i, i ^ j) for i in range(seqs)],
        )
        for j in range(1, seqs)
    ]


def solution(mesh):
    placed = (
        P("bucket", "seq", None),
        P("bucket", "seq", None),
        P("bucket", None),
        P("bucket"),
        P("bucket", None),
        P("bucket", None),
        P("bucket", None, None),
        P("bucket", None, None),
        P("bucket", "seq"),
        P(),
        P("bucket", "seq"),
        P("seq"),
        P(),
        P(),
        P(),
        P(),
        P(),
        P(),
        P(),
        P(),
        P(),
    )
    return jax.shard_map(
        body,
        mesh=mesh,
        in_specs=placed,
        out_specs=(
            P("bucket", "seq", None),
            P("bucket", "seq", None),
            P(None, "bucket"),
            P("bucket", "seq"),
            P("seq", "bucket"),
            P(None, "bucket"),
            P("bucket"),
            P(None, "bucket"),
            P("bucket"),
            P(None, "bucket"),
            P("bucket"),
            P("bucket", None),
            P("bucket"),
            P("bucket"),
        ),
        check_vma=False,
    )
```
